256 devices in a mesh: energy: 16 (over z, core), cell: 16 (over y, x).
Axes of the slice: x: 4, y: 4, z: 8, core: 2. Of those that a mesh axis runs over, the one named last changes fastest.
Arguments:
- green: bfloat16 [4, 96, 32, 16, 512], P(None, 'energy', 'cell'), may hold values from -6 to 6
- screened: bfloat16 [4, 96, 32, 16, 512], P(None, 'energy', None, 'cell'), may hold values from -6 to 6
- cell_map: int32 [32], replicated, may hold values from 0 to 31, each once
- shift_table: int32 [16, 16, 3], replicated, may hold values from 0 to 5, as said below
- shift_count: int32 [16, 16], replicated, may hold values from 1 to 3, as said below
Outputs:
- sigma: float32 [4, 96, 32, 16, 512], P(None, 'energy', 'cell')
The draws below stay inside these ranges and needn't reach their ends.
Inputs may be any that keep to these rules, and one draw needn't show every extreme that they name: `shift_table`: offsets of requested energies within the source group; slots c >= shift_count[g, s] are not read. `shift_count`: some destination group requests 3 energies from every source group. `cell_map`: each cell stands at exactly one position.
All inputs are finite; a program needn't handle non-finite values.
Results may differ from the reference program's by a relative error of at most 0.0003.
Values may be sent and summed in bfloat16 or wider, within the bound.
A program may use at most 128 MiB of HBM per device.

```python
import jax
import jax.numpy as jnp
from jax import lax

B = 512
R = 16
E_DEV = 6
CAP = 3
NG = 16
NE = 96
NC = 32


def draw_shift_table(key, part):
    return jax.random.randint(key, (NG, NG, CAP), 0, E_DEV, dtype=jnp.int32)


def draw_shift_count(key, part):
    first_key, second_key = jax.random.split(key)
    base = jax.random.randint(first_key, (NG, NG), 1, CAP + 1, dtype=jnp.int32)
    full_row = jax.random.randint(second_key, (), 0, NG, dtype=jnp.int32)
    rows = lax.broadcasted_iota(jnp.int32, (NG, NG), 0)
    return jnp.where(rows == full_row, jnp.int32(CAP), base)


def block_levels(key, shape, shards, low, high):
    gain, own = 1.0, jax.random.fold_in(key, 6)
    for dim, parts in shards:
        steps = jnp.exp(jax.random.uniform(jax.random.fold_in(own, dim), (parts,), jnp.float32, low / len(shards), high / len(shards)))
        gain = gain * jnp.repeat(steps, shape[dim] // parts).reshape([-1 if axis == dim else 1 for axis in range(len(shape))])
    return gain


def bell_draw(stream_key, shape, width, most, cuts=(), held_as=jnp.bfloat16):
    result = jax.random.normal(stream_key, shape, jnp.float32) * width
    if len(cuts) > 0:
        result = block_levels(stream_key, shape, cuts, -0.22, 0.18) * result
    return jnp.clip(result, min=-most, max=most).astype(held_as)


def setup_inputs(seed: int = 0) -> dict:
    splits = jax.random.split(jax.random.key(seed), 6)
    green = bell_draw(splits[0], (4, NE, NC, R, B), 1.0, 6.0, ((1, 16), (2, 16)))
    screened = bell_draw(splits[1], (4, NE, NC, R, B), 1.0, 6.0, ((1, 16), (3, 16)))
    cell_map = jax.random.permutation(splits[2], NC).astype(jnp.int32)
    shift_table = draw_shift_table(jax.random.fold_in(splits[5], 71), 0)
    shift_count = draw_shift_count(jax.random.fold_in(splits[5], 71), 0)
    return {"green": green, "screened": screened, "cell_map": cell_map, "shift_table": shift_table, "shift_count": shift_count}


SCALE = 0.2


def complex_terms(windows, values):
    g_real = windows[:, 0::2]
    g_imag = windows[:, 1::2]
    w_real = values[:, 0::2]
    w_imag = values[:, 1::2]
    real_part = -(g_real * w_imag + g_imag * w_real)
    imag_part = g_real * w_real - g_imag * w_imag
    stacked = jnp.stack([real_part, imag_part], axis=2)
    return stacked.reshape((stacked.shape[0], 4) + stacked.shape[3:])


def reference(green, screened, cell_map, shift_table, shift_count):
    owned = jnp.take(screened, cell_map, axis=2)
    padding = jnp.zeros((4, E_DEV) + green.shape[2:], green.dtype)
    padded = jnp.concatenate([padding, green], axis=1)
    slots = jnp.arange(CAP, dtype=jnp.int32)

    def one_group(group):
        first = (group * E_DEV).astype(jnp.int32)
        table_row = shift_table[group]
        counts = shift_count[group]

        def turn(total, source):
            energies = (source * E_DEV + table_row[source]).astype(jnp.int32)
            live = (slots < counts[source]).astype(jnp.float32)
            starts = (jnp.maximum(first - energies, -E_DEV) + E_DEV).astype(jnp.int32)
            windows = jax.vmap(lambda begin: lax.dynamic_slice_in_dim(padded, begin, E_DEV, 1))(starts)
            values = jnp.moveaxis(jnp.take(owned, energies, axis=1), 1, 0)
            terms = complex_terms(windows.astype(jnp.float32), values.astype(jnp.float32)[:, :, None])
            return total + jnp.sum(terms * live[:, None, None, None, None, None], axis=0), None

        zeros = jnp.zeros((4, E_DEV, NC, R, B), jnp.float32)
        total, _ = lax.scan(turn, zeros, jnp.arange(NG, dtype=jnp.int32))
        return total * SCALE

    blocks = lax.map(one_group, jnp.arange(NG, dtype=jnp.int32))
    return jnp.moveaxis(blocks, 0, 1).reshape(4, NE, NC, R, B)
```

```python
import functools

import jax
import jax.numpy as jnp
from jax import lax
from jax.experimental import pallas as pl
from jax.experimental.pallas import tpu as pltpu
from jax.sharding import PartitionSpec as P

SCALE = 0.2
LANES = 128


def term_lists(shift_table, shift_count, group, per_energy):
    groups, slot_count = shift_table.shape[1], shift_table.shape[2]
    total = groups * slot_count
    base = group * per_energy
    table_row = shift_table[group]
    counts = shift_count[group]
    source = lax.broadcasted_iota(jnp.int32, (groups, slot_count), 0)
    slot = lax.broadcasted_iota(jnp.int32, (groups, slot_count), 1)
    energies = (source * per_energy + table_row).reshape(total)
    live = (slot < counts[:, None]).reshape(total)
    local = lax.broadcasted_iota(jnp.int32, (per_energy, 1), 0)
    valid = live[None, :] & (energies[None, :] <= base + local)
    place = jnp.cumsum(valid.astype(jnp.int32), axis=1) - 1
    target = lax.broadcasted_iota(jnp.int32, (1, 1, total), 2)
    hit = valid[:, :, None] & (place[:, :, None] == target)
    lists = jnp.sum(jnp.where(hit, energies[None, :, None], 0), axis=1)
    sizes = jnp.sum(valid.astype(jnp.int32), axis=1)
    head = jnp.concatenate([sizes, base[None]]).astype(jnp.int32)
    return head, lists.reshape(-1).astype(jnp.int32)


def conv_kernel(per_energy, total, head_ref, lists_ref, g_ref, w_ref, o_ref):
    base = head_ref[per_energy]
    rows, width = g_ref.shape[2], g_ref.shape[3]
    for chunk in range(width // LANES):
        lanes = pl.ds(chunk * LANES, LANES)
        for e in range(per_energy):
            def body(t, acc, e=e, lanes=lanes):
                w = lists_ref[e * total + t]
                u = base + e - w
                out = list(acc)
                for kind in range(2):
                    gr = g_ref[2 * kind, u, :, lanes].astype(jnp.float32)
                    gi = g_ref[2 * kind + 1, u, :, lanes].astype(jnp.float32)
                    wr = w_ref[2 * kind, w, :, lanes].astype(jnp.float32)
                    wi = w_ref[2 * kind + 1, w, :, lanes].astype(jnp.float32)
                    out[2 * kind] = out[2 * kind] - (gr * wi + gi * wr)
                    out[2 * kind + 1] = out[2 * kind + 1] + (gr * wr - gi * wi)
                return tuple(out)

            zero = jnp.zeros((rows, LANES), jnp.float32)
            acc = lax.fori_loop(0, head_ref[e], body, (zero,) * 4)
            for comp in range(4):
                o_ref[comp, e, :, lanes] = acc[comp] * SCALE


def convolve(head, lists, whole, every, per_energy):
    comps, energies, positions, rows, width = whole.shape
    total = lists.shape[0] // per_energy
    in_block = pl.BlockSpec(
        (comps, energies, pl.squeezed, rows, width), lambda p, h, l: (0, 0, p, 0, 0)
    )
    out_block = pl.BlockSpec(
        (comps, per_energy, pl.squeezed, rows, width), lambda p, h, l: (0, 0, p, 0, 0)
    )
    return pl.pallas_call(
        functools.partial(conv_kernel, per_energy, total),
        out_shape=jax.ShapeDtypeStruct((comps, per_energy, positions, rows, width), jnp.float32),
        grid_spec=pltpu.PrefetchScalarGridSpec(
            num_scalar_prefetch=2,
            grid=(positions,),
            in_specs=[in_block, in_block],
            out_specs=out_block,
        ),
        compiler_params=pltpu.CompilerParams(vmem_limit_bytes=48 * 1024 * 1024),
    )(head, lists, whole, every)


def per_device(green, screened, cell_map, shift_table, shift_count):
    cell_count = lax.axis_size("cell")
    per_energy = green.shape[1]
    per_cell = green.shape[2]
    width = green.shape[4]
    wanted = jnp.transpose(cell_map.reshape(cell_count, per_cell)).reshape(-1)
    outgoing = jnp.take(screened, wanted, axis=2)
    outgoing = outgoing.reshape(4, per_energy, per_cell, cell_count, screened.shape[3], width)
    arrived = lax.all_to_all(outgoing, "cell", split_axis=3, concat_axis=3, tiled=True)
    owned = arrived.reshape(4, per_energy, per_cell, green.shape[3], width)
    whole = lax.all_gather(green, "energy", axis=1, tiled=True)
    every = lax.all_gather(owned, "energy", axis=1, tiled=True)
    group = lax.axis_index("energy")
    head, lists = term_lists(shift_table, shift_count, group, per_energy)
    return convolve(head, lists, whole, every, per_energy)


def solution(mesh):
    placed = (
        P(None, "energy", "cell", None, None),
        P(None, "energy", None, "cell", None),
        P(),
        P(),
        P(),
    )
    return jax.shard_map(
        per_device,
        mesh=mesh,
        in_specs=placed,
        out_specs=P(None, "energy", "cell", None, None),
        check_vma=False,
    )
```

```python
import functools

import jax
import jax.numpy as jnp
from jax import lax
from jax.experimental import pallas as pl
from jax.experimental.pallas import tpu as pltpu
from jax.sharding import PartitionSpec as P

SCALE = 0.2
LANES = 128


def term_lists(shift_table, shift_count, group, per_energy):
    groups, slot_count = shift_table.shape[1], shift_table.shape[2]
    total = groups * slot_count
    base = group * per_energy
    table_row = shift_table[group]
    counts = shift_count[group]
    source = lax.broadcasted_iota(jnp.int32, (groups, slot_count), 0)
    slot = lax.broadcasted_iota(jnp.int32, (groups, slot_count), 1)
    energies = (source * per_energy + table_row).reshape(total)
    live = (slot < counts[:, None]).reshape(total)
    local = lax.broadcasted_iota(jnp.int32, (per_energy, 1), 0)
    valid = live[None, :] & (energies[None, :] <= base + local)
    place = jnp.cumsum(valid.astype(jnp.int32), axis=1) - 1
    target = lax.broadcasted_iota(jnp.int32, (1, 1, total), 2)
    hit = valid[:, :, None] & (place[:, :, None] == target)
    lists = jnp.sum(jnp.where(hit, energies[None, :, None], 0), axis=1)
    sizes = jnp.sum(valid.astype(jnp.int32), axis=1)
    head = jnp.concatenate([sizes, base[None]]).astype(jnp.int32)
    slots = jnp.remainder(group - lists // per_energy, groups)
    places = slots * per_energy + jnp.remainder(lists, per_energy)
    return head, lists.reshape(-1).astype(jnp.int32), places.reshape(-1).astype(jnp.int32)


def conv_kernel(per_energy, total, head_ref, lists_ref, places_ref, g_ref, w_ref, o_ref):
    base = head_ref[per_energy]
    rows, width = g_ref.shape[2], g_ref.shape[3]
    for chunk in range(width // LANES):
        lanes = pl.ds(chunk * LANES, LANES)
        for e in range(per_energy):
            def body(t, acc, e=e, lanes=lanes):
                w = lists_ref[e * total + t]
                u = base + e - w
                v = places_ref[e * total + t]
                out = list(acc)
                for kind in range(2):
                    gr = g_ref[2 * kind, u, :, lanes].astype(jnp.float32)
                    gi = g_ref[2 * kind + 1, u, :, lanes].astype(jnp.float32)
                    wr = w_ref[2 * kind, v, :, lanes].astype(jnp.float32)
                    wi = w_ref[2 * kind + 1, v, :, lanes].astype(jnp.float32)
                    out[2 * kind] = out[2 * kind] - (gr * wi + gi * wr)
                    out[2 * kind + 1] = out[2 * kind + 1] + (gr * wr - gi * wi)
                return tuple(out)

            zero = jnp.zeros((rows, LANES), jnp.float32)
            acc = lax.fori_loop(0, head_ref[e], body, (zero,) * 4)
            for comp in range(4):
                o_ref[comp, e, :, lanes] = acc[comp] * SCALE


def convolve(head, lists, places, whole, every, per_energy):
    comps, energies, positions, rows, width = whole.shape
    total = lists.shape[0] // per_energy
    in_block = pl.BlockSpec(
        (comps, energies, pl.squeezed, rows, width), lambda p, *_: (0, 0, p, 0, 0)
    )
    out_block = pl.BlockSpec(
        (comps, per_energy, pl.squeezed, rows, width), lambda p, *_: (0, 0, p, 0, 0)
    )
    return pl.pallas_call(
        functools.partial(conv_kernel, per_energy, total),
        out_shape=jax.ShapeDtypeStruct((comps, per_energy, positions, rows, width), jnp.float32),
        grid_spec=pltpu.PrefetchScalarGridSpec(
            num_scalar_prefetch=3,
            grid=(positions,),
            in_specs=[in_block, in_block],
            out_specs=out_block,
        ),
        compiler_params=pltpu.CompilerParams(vmem_limit_bytes=48 * 1024 * 1024),
    )(head, lists, places, whole, every)


def per_device(green, screened, cell_map, shift_table, shift_count):
    cell_count = lax.axis_size("cell")
    per_energy = green.shape[1]
    per_cell = green.shape[2]
    width = green.shape[4]
    wanted = jnp.transpose(cell_map.reshape(cell_count, per_cell)).reshape(-1)
    outgoing = jnp.take(screened, wanted, axis=2)
    outgoing = outgoing.reshape(4, per_energy, per_cell, cell_count, screened.shape[3], width)
    arrived = lax.all_to_all(outgoing, "cell", split_axis=3, concat_axis=3, tiled=True)
    owned = arrived.reshape(4, per_energy, per_cell, green.shape[3], width)
    whole = lax.all_gather(green, "energy", axis=1, tiled=True)
    every = ring_gather(owned, "energy")
    group = lax.axis_index("energy")
    head, lists, places = term_lists(shift_table, shift_count, group, per_energy)
    return convolve(head, lists, places, whole, every, per_energy)


def ring_gather(block, axis):
    n = lax.axis_size(axis)
    forward = [(i, (i + 1) % n) for i in range(n)]
    backward = [(i, (i - 1) % n) for i in range(n)]
    ahead, behind = block, block
    near, far = [], []
    for step in range(1, n // 2 + 1):
        ahead = lax.ppermute(ahead, axis, forward)
        near.append(ahead)
        if step < n - n // 2:
            behind = lax.ppermute(behind, axis, backward)
            far.append(behind)
    return jnp.concatenate([block] + near + far[::-1], axis=1)


def solution(mesh):
    placed = (
        P(None, "energy", "cell", None, None),
        P(None, "energy", None, "cell", None),
        P(),
        P(),
        P(),
    )
    return jax.shard_map(
        per_device,
        mesh=mesh,
        in_specs=placed,
        out_specs=P(None, "energy", "cell", None, None),
        check_vma=False,
    )
```

```python
import functools

import jax
import jax.numpy as jnp
from jax import lax
from jax.experimental import pallas as pl
from jax.experimental.pallas import tpu as pltpu
from jax.sharding import PartitionSpec as P

SCALE = 0.2
LANES = 128


def term_lists(shift_table, shift_count, group, per_energy):
    groups, slot_count = shift_table.shape[1], shift_table.shape[2]
    total = groups * slot_count
    base = group * per_energy
    table_row = shift_table[group]
    counts = shift_count[group]
    source = lax.broadcasted_iota(jnp.int32, (groups, slot_count), 0)
    slot = lax.broadcasted_iota(jnp.int32, (groups, slot_count), 1)
    energies = (source * per_energy + table_row).reshape(total)
    live = (slot < counts[:, None]).reshape(total)
    local = lax.broadcasted_iota(jnp.int32, (per_energy, 1), 0)
    valid = live[None, :] & (energies[None, :] <= base + local)
    place = jnp.cumsum(valid.astype(jnp.int32), axis=1) - 1
    target = lax.broadcasted_iota(jnp.int32, (1, 1, total), 2)
    hit = valid[:, :, None] & (place[:, :, None] == target)
    lists = jnp.sum(jnp.where(hit, energies[None, :, None], 0), axis=1)
    sizes = jnp.sum(valid.astype(jnp.int32), axis=1)
    head = jnp.concatenate([sizes, base[None]]).astype(jnp.int32)
    return head, lists.reshape(-1).astype(jnp.int32)


def conv_kernel(per_energy, total, head_ref, lists_ref, x_ref, o_ref):
    base = head_ref[per_energy]
    rows, width = x_ref.shape[4], x_ref.shape[5]
    for chunk in range(width // LANES):
        lanes = pl.ds(chunk * LANES, LANES)
        for e in range(per_energy):
            def body(t, acc, e=e, lanes=lanes):
                w = lists_ref[e * total + t]
                u = base + e - w
                ug, uo = u // per_energy, u % per_energy
                wg, wo = w // per_energy, w % per_energy
                out = list(acc)
                for kind in range(2):
                    gr = x_ref[ug, 0, 2 * kind, uo, :, lanes].astype(jnp.float32)
                    gi = x_ref[ug, 0, 2 * kind + 1, uo, :, lanes].astype(jnp.float32)
                    wr = x_ref[wg, 1, 2 * kind, wo, :, lanes].astype(jnp.float32)
                    wi = x_ref[wg, 1, 2 * kind + 1, wo, :, lanes].astype(jnp.float32)
                    out[2 * kind] = out[2 * kind] - (gr * wi + gi * wr)
                    out[2 * kind + 1] = out[2 * kind + 1] + (gr * wr - gi * wi)
                return tuple(out)

            zero = jnp.zeros((rows, LANES), jnp.float32)
            acc = lax.fori_loop(0, head_ref[e], body, (zero,) * 4)
            for comp in range(4):
                o_ref[comp, e, :, lanes] = acc[comp] * SCALE


def convolve(head, lists, stacked, per_energy):
    groups, pair, comps, _, positions, rows, width = stacked.shape
    total = lists.shape[0] // per_energy
    in_block = pl.BlockSpec(
        (groups, pair, comps, per_energy, pl.squeezed, rows, width),
        lambda p, h, l: (0, 0, 0, 0, p, 0, 0),
    )
    out_block = pl.BlockSpec(
        (comps, per_energy, pl.squeezed, rows, width), lambda p, h, l: (0, 0, p, 0, 0)
    )
    return pl.pallas_call(
        functools.partial(conv_kernel, per_energy, total),
        out_shape=jax.ShapeDtypeStruct((comps, per_energy, positions, rows, width), jnp.float32),
        grid_spec=pltpu.PrefetchScalarGridSpec(
            num_scalar_prefetch=2,
            grid=(positions,),
            in_specs=[in_block],
            out_specs=out_block,
        ),
        compiler_params=pltpu.CompilerParams(vmem_limit_bytes=48 * 1024 * 1024),
    )(head, lists, stacked)


def per_device(green, screened, cell_map, shift_table, shift_count):
    cell_count = lax.axis_size("cell")
    per_energy = green.shape[1]
    per_cell = green.shape[2]
    width = green.shape[4]
    wanted = jnp.transpose(cell_map.reshape(cell_count, per_cell)).reshape(-1)
    outgoing = jnp.take(screened, wanted, axis=2)
    outgoing = outgoing.reshape(4, per_energy, per_cell, cell_count, screened.shape[3], width)
    arrived = lax.all_to_all(outgoing, "cell", split_axis=3, concat_axis=3, tiled=True)
    owned = arrived.reshape(4, per_energy, per_cell, green.shape[3], width)
    stacked = gather_energy(jnp.stack([green, owned]))
    group = lax.axis_index("energy")
    head, lists = term_lists(shift_table, shift_count, group, per_energy)
    return convolve(head, lists, stacked, per_energy)


def gather_kernel(chips, x_ref, out_ref, local_sem, ring_send, ring_recv, pass_send, pass_recv):
    me = lax.axis_index("energy")
    cell = lax.axis_index("cell")
    chip, core = me // 2, me % 2
    step_dir = 1 - 2 * core
    partner = me + step_dir
    ahead = 2 * ((chip + step_dir + chips) % chips) + core

    def origin(k):
        return 2 * ((chip - step_dir * k + chips) % chips) + core

    def ring_copy(k):
        slot = origin(k - 1)
        src = x_ref if k == 1 else out_ref.at[slot]
        return pltpu.make_async_remote_copy(
            src_ref=src, dst_ref=out_ref.at[slot],
            send_sem=ring_send.at[k], recv_sem=ring_recv.at[k],
            device_id=(ahead, cell), device_id_type=pl.DeviceIdType.MESH,
        )

    def pass_copy(k):
        slot = origin(k)
        src = x_ref if k == 0 else out_ref.at[slot]
        return pltpu.make_async_remote_copy(
            src_ref=src, dst_ref=out_ref.at[slot],
            send_sem=pass_send.at[k], recv_sem=pass_recv.at[k],
            device_id=(partner, cell), device_id_type=pl.DeviceIdType.MESH,
        )

    def arrival(k):
        slot = origin(k)
        return pltpu.make_async_remote_copy(
            src_ref=out_ref.at[slot], dst_ref=out_ref.at[slot],
            send_sem=ring_send.at[k], recv_sem=ring_recv.at[k],
            device_id=(ahead, cell), device_id_type=pl.DeviceIdType.MESH,
        )

    def handed(k):
        slot = 2 * ((chip + step_dir * k + chips) % chips) + 1 - core
        return pltpu.make_async_remote_copy(
            src_ref=out_ref.at[slot], dst_ref=out_ref.at[slot],
            send_sem=pass_send.at[k], recv_sem=pass_recv.at[k],
            device_id=(partner, cell), device_id_type=pl.DeviceIdType.MESH,
        )

    local = pltpu.make_async_copy(x_ref, out_ref.at[me], local_sem)
    local.start()
    sends = [ring_copy(1), pass_copy(0)]
    for copy in sends:
        copy.start()
    for k in range(1, chips):
        arrival(k).wait_recv()
        onward = [pass_copy(k)]
        if k + 1 < chips:
            onward.append(ring_copy(k + 1))
        for copy in onward:
            copy.start()
        sends.extend(onward)
    for k in range(chips):
        handed(k).wait_recv()
    for copy in sends:
        copy.wait_send()
    local.wait()


def gather_energy(block):
    groups = lax.axis_size("energy")
    chips = groups // 2
    return pl.pallas_call(
        functools.partial(gather_kernel, chips),
        out_shape=jax.ShapeDtypeStruct((groups,) + block.shape, block.dtype),
        in_specs=[pl.BlockSpec(memory_space=pl.ANY)],
        out_specs=pl.BlockSpec(memory_space=pl.ANY),
        scratch_shapes=[
            pltpu.SemaphoreType.DMA(()),
            pltpu.SemaphoreType.DMA((chips,)),
            pltpu.SemaphoreType.DMA((chips,)),
            pltpu.SemaphoreType.DMA((chips,)),
            pltpu.SemaphoreType.DMA((chips,)),
        ],
        compiler_params=pltpu.CompilerParams(has_side_effects=True),
    )(block)


def solution(mesh):
    placed = (
        P(None, "energy", "cell", None, None),
        P(None, "energy", None, "cell", None),
        P(),
        P(),
        P(),
    )
    return jax.shard_map(
        per_device,
        mesh=mesh,
        in_specs=placed,
        out_specs=P(None, "energy", "cell", None, None),
        check_vma=False,
    )
```

```python
import functools

import jax
import jax.numpy as jnp
from jax import lax
from jax.experimental import pallas as pl
from jax.experimental.pallas import tpu as pltpu
from jax.sharding import PartitionSpec as P

SCALE = 0.2
LANES = 128


def term_lists(shift_table, shift_count, group, per_energy):
    groups, slot_count = shift_table.shape[1], shift_table.shape[2]
    total = groups * slot_count
    base = group * per_energy
    table_row = shift_table[group]
    counts = shift_count[group]
    source = lax.broadcasted_iota(jnp.int32, (groups, slot_count), 0)
    slot = lax.broadcasted_iota(jnp.int32, (groups, slot_count), 1)
    energies = (source * per_energy + table_row).reshape(total)
    live = (slot < counts[:, None]).reshape(total)
    local = lax.broadcasted_iota(jnp.int32, (per_energy, 1), 0)
    valid = live[None, :] & (energies[None, :] <= base + local)
    place = jnp.cumsum(valid.astype(jnp.int32), axis=1) - 1
    target = lax.broadcasted_iota(jnp.int32, (1, 1, total), 2)
    hit = valid[:, :, None] & (place[:, :, None] == target)
    lists = jnp.sum(jnp.where(hit, energies[None, :, None], 0), axis=1)
    sizes = jnp.sum(valid.astype(jnp.int32), axis=1)
    head = jnp.concatenate([sizes, base[None]]).astype(jnp.int32)
    return head, lists.reshape(-1).astype(jnp.int32)


def conv_kernel(per_energy, total, head_ref, lists_ref, g_ref, w_ref, o_ref, gf, wf):
    base = head_ref[per_energy]
    rows, width = g_ref.shape[2], g_ref.shape[3]
    comps = g_ref.shape[0]
    held = base // per_energy + 1
    for chunk in range(width // LANES):
        lanes = pl.ds(chunk * LANES, LANES)

        def widen(grp, carry, lanes=lanes):
            energies = pl.ds(grp * per_energy, per_energy)
            for comp in range(comps):
                gf[comp, energies] = g_ref[comp, energies, :, lanes].astype(jnp.float32)
                wf[comp, energies] = w_ref[comp, energies, :, lanes].astype(jnp.float32)
            return carry

        lax.fori_loop(0, held, widen, 0)
        for e in range(per_energy):
            def body(t, acc, e=e):
                w = lists_ref[e * total + t]
                u = base + e - w
                out = list(acc)
                for kind in range(2):
                    gr = gf[2 * kind, u]
                    gi = gf[2 * kind + 1, u]
                    wr = wf[2 * kind, w]
                    wi = wf[2 * kind + 1, w]
                    out[2 * kind] = out[2 * kind] - (gr * wi + gi * wr)
                    out[2 * kind + 1] = out[2 * kind + 1] + (gr * wr - gi * wi)
                return tuple(out)

            zero = jnp.zeros((rows, LANES), jnp.float32)
            acc = lax.fori_loop(0, head_ref[e], body, (zero,) * 4)
            for comp in range(comps):
                o_ref[comp, e, :, lanes] = acc[comp] * SCALE


def convolve(head, lists, whole, every, per_energy):
    comps, energies, positions, rows, width = whole.shape
    total = lists.shape[0] // per_energy
    in_block = pl.BlockSpec(
        (comps, energies, pl.squeezed, rows, width), lambda p, h, l: (0, 0, p, 0, 0)
    )
    out_block = pl.BlockSpec(
        (comps, per_energy, pl.squeezed, rows, width), lambda p, h, l: (0, 0, p, 0, 0)
    )
    return pl.pallas_call(
        functools.partial(conv_kernel, per_energy, total),
        out_shape=jax.ShapeDtypeStruct((comps, per_energy, positions, rows, width), jnp.float32),
        grid_spec=pltpu.PrefetchScalarGridSpec(
            num_scalar_prefetch=2,
            grid=(positions,),
            in_specs=[in_block, in_block],
            out_specs=out_block,
            scratch_shapes=[
                pltpu.VMEM((comps, energies, rows, LANES), jnp.float32),
                pltpu.VMEM((comps, energies, rows, LANES), jnp.float32),
            ],
        ),
        compiler_params=pltpu.CompilerParams(vmem_limit_bytes=48 * 1024 * 1024),
    )(head, lists, whole, every)


def per_device(green, screened, cell_map, shift_table, shift_count):
    cell_count = lax.axis_size("cell")
    per_energy = green.shape[1]
    per_cell = green.shape[2]
    width = green.shape[4]
    wanted = jnp.transpose(cell_map.reshape(cell_count, per_cell)).reshape(-1)
    outgoing = jnp.take(screened, wanted, axis=2)
    outgoing = outgoing.reshape(4, per_energy, per_cell, cell_count, screened.shape[3], width)
    arrived = lax.all_to_all(outgoing, "cell", split_axis=3, concat_axis=3, tiled=True)
    owned = arrived.reshape(4, per_energy, per_cell, green.shape[3], width)
    whole = lax.all_gather(green, "energy", axis=1, tiled=True)
    every = lax.all_gather(owned, "energy", axis=1, tiled=True)
    group = lax.axis_index("energy")
    head, lists = term_lists(shift_table, shift_count, group, per_energy)
    return convolve(head, lists, whole, every, per_energy)


def solution(mesh):
    placed = (
        P(None, "energy", "cell", None, None),
        P(None, "energy", None, "cell", None),
        P(),
        P(),
        P(),
    )
    return jax.shard_map(
        per_device,
        mesh=mesh,
        in_specs=placed,
        out_specs=P(None, "energy", "cell", None, None),
        check_vma=False,
    )
```

```python
import functools

import jax
import jax.numpy as jnp
from jax import lax
from jax.experimental import pallas as pl
from jax.experimental.pallas import tpu as pltpu
from jax.sharding import PartitionSpec as P

SCALE = 0.2
LANES = 128
CHUNK = 128


def term_lists(shift_table, shift_count, group, per_energy):
    groups, slot_count = shift_table.shape[1], shift_table.shape[2]
    total = groups * slot_count
    base = group * per_energy
    table_row = shift_table[group]
    counts = shift_count[group]
    source = lax.broadcasted_iota(jnp.int32, (groups, slot_count), 0)
    slot = lax.broadcasted_iota(jnp.int32, (groups, slot_count), 1)
    energies = (source * per_energy + table_row).reshape(total)
    live = (slot < counts[:, None]).reshape(total)
    local = lax.broadcasted_iota(jnp.int32, (per_energy, 1), 0)
    valid = live[None, :] & (energies[None, :] <= base + local)
    place = jnp.cumsum(valid.astype(jnp.int32), axis=1) - 1
    target = lax.broadcasted_iota(jnp.int32, (1, 1, total), 2)
    hit = valid[:, :, None] & (place[:, :, None] == target)
    lists = jnp.sum(jnp.where(hit, energies[None, :, None], 0), axis=1)
    sizes = jnp.sum(valid.astype(jnp.int32), axis=1)
    head = jnp.concatenate([sizes, base[None]]).astype(jnp.int32)
    return head, lists.reshape(-1).astype(jnp.int32)


def conv_kernel(per_energy, total, head_ref, lists_ref, g_ref, w_ref, o_ref):
    base = head_ref[per_energy]
    rows, width = g_ref.shape[2], g_ref.shape[3]
    for chunk in range(width // LANES):
        lanes = pl.ds(chunk * LANES, LANES)
        for e in range(per_energy):
            def body(t, acc, e=e, lanes=lanes):
                w = lists_ref[e * total + t]
                u = base + e - w
                out = list(acc)
                for kind in range(2):
                    gr = g_ref[2 * kind, u, :, lanes].astype(jnp.float32)
                    gi = g_ref[2 * kind + 1, u, :, lanes].astype(jnp.float32)
                    wr = w_ref[2 * kind, w, :, lanes].astype(jnp.float32)
                    wi = w_ref[2 * kind + 1, w, :, lanes].astype(jnp.float32)
                    out[2 * kind] = out[2 * kind] - (gr * wi + gi * wr)
                    out[2 * kind + 1] = out[2 * kind + 1] + (gr * wr - gi * wi)
                return tuple(out)

            zero = jnp.zeros((rows, LANES), jnp.float32)
            acc = lax.fori_loop(0, head_ref[e], body, (zero,) * 4)
            for comp in range(4):
                o_ref[comp, e, :, lanes] = acc[comp] * SCALE


def convolve(head, lists, whole, every, per_energy):
    comps, energies, positions, rows, width = whole.shape
    total = lists.shape[0] // per_energy
    in_block = pl.BlockSpec(
        (comps, energies, pl.squeezed, rows, width), lambda p, h, l: (0, 0, p, 0, 0)
    )
    out_block = pl.BlockSpec(
        (comps, per_energy, pl.squeezed, rows, width), lambda p, h, l: (0, 0, p, 0, 0)
    )
    return pl.pallas_call(
        functools.partial(conv_kernel, per_energy, total),
        out_shape=jax.ShapeDtypeStruct((comps, per_energy, positions, rows, width), jnp.float32),
        grid_spec=pltpu.PrefetchScalarGridSpec(
            num_scalar_prefetch=2,
            grid=(positions,),
            in_specs=[in_block, in_block],
            out_specs=out_block,
        ),
        compiler_params=pltpu.CompilerParams(vmem_limit_bytes=48 * 1024 * 1024),
    )(head, lists, whole, every)


def per_device(green, screened, cell_map, shift_table, shift_count):
    cell_count = lax.axis_size("cell")
    per_energy = green.shape[1]
    per_cell = green.shape[2]
    width = green.shape[4]
    wanted = jnp.transpose(cell_map.reshape(cell_count, per_cell)).reshape(-1)
    outgoing = jnp.take(screened, wanted, axis=2)
    outgoing = outgoing.reshape(4, per_energy, per_cell, cell_count, screened.shape[3], width)
    arrived = lax.all_to_all(outgoing, "cell", split_axis=3, concat_axis=3, tiled=True)
    owned = arrived.reshape(4, per_energy, per_cell, green.shape[3], width)
    group = lax.axis_index("energy")
    head, lists = term_lists(shift_table, shift_count, group, per_energy)
    parts = []
    for start in range(0, width, CHUNK):
        lanes = slice(start, start + CHUNK)
        whole = lax.all_gather(green[..., lanes], "energy", axis=1, tiled=True)
        every = lax.all_gather(owned[..., lanes], "energy", axis=1, tiled=True)
        parts.append(convolve(head, lists, whole, every, per_energy))
    return jnp.concatenate(parts, axis=-1)


def solution(mesh):
    placed = (
        P(None, "energy", "cell", None, None),
        P(None, "energy", None, "cell", None),
        P(),
        P(),
        P(),
    )
    return jax.shard_map(
        per_device,
        mesh=mesh,
        in_specs=placed,
        out_specs=P(None, "energy", "cell", None, None),
        check_vma=False,
    )
```

```python
import functools

import jax
import jax.numpy as jnp
from jax import lax
from jax.experimental import pallas as pl
from jax.experimental.pallas import tpu as pltpu
from jax.sharding import PartitionSpec as P

SCALE = 0.2
LANES = 128


def term_lists(shift_table, shift_count, group, per_energy):
    groups, slot_count = shift_table.shape[1], shift_table.shape[2]
    total = groups * slot_count
    base = group * per_energy
    table_row = shift_table[group]
    counts = shift_count[group]
    source = lax.broadcasted_iota(jnp.int32, (groups, slot_count), 0)
    slot = lax.broadcasted_iota(jnp.int32, (groups, slot_count), 1)
    energies = (source * per_energy + table_row).reshape(total)
    live = (slot < counts[:, None]).reshape(total)
    local = lax.broadcasted_iota(jnp.int32, (per_energy, 1), 0)
    valid = live[None, :] & (energies[None, :] <= base + local)
    place = jnp.cumsum(valid.astype(jnp.int32), axis=1) - 1
    target = lax.broadcasted_iota(jnp.int32, (1, 1, total), 2)
    hit = valid[:, :, None] & (place[:, :, None] == target)
    lists = jnp.sum(jnp.where(hit, energies[None, :, None], 0), axis=1)
    sizes = jnp.sum(valid.astype(jnp.int32), axis=1)
    head = jnp.concatenate([sizes, base[None]]).astype(jnp.int32)
    return head, lists.reshape(-1).astype(jnp.int32)


def conv_kernel(per_energy, total, head_ref, lists_ref, g_ref, w_ref, o_ref):
    base = head_ref[per_energy]
    rows, width = g_ref.shape[2], g_ref.shape[3]
    for chunk in range(width // LANES):
        lanes = pl.ds(chunk * LANES, LANES)
        for e in range(per_energy):
            def term(t, acc, e=e, lanes=lanes):
                w = lists_ref[e * total + t]
                u = base + e - w
                out = list(acc)
                for kind in range(2):
                    gr = g_ref[2 * kind, u, :, lanes].astype(jnp.float32)
                    gi = g_ref[2 * kind + 1, u, :, lanes].astype(jnp.float32)
                    wr = w_ref[2 * kind, w, :, lanes].astype(jnp.float32)
                    wi = w_ref[2 * kind + 1, w, :, lanes].astype(jnp.float32)
                    out[2 * kind] = out[2 * kind] - (gr * wi + gi * wr)
                    out[2 * kind + 1] = out[2 * kind + 1] + (gr * wr - gi * wi)
                return tuple(out)

            def pair(i, accs):
                return term(2 * i, accs[0]), term(2 * i + 1, accs[1])

            count = head_ref[e]
            zero = (jnp.zeros((rows, LANES), jnp.float32),) * 4
            first, second = lax.fori_loop(0, count // 2, pair, (zero, zero))
            first = lax.fori_loop(2 * (count // 2), count, term, first)
            for comp in range(4):
                o_ref[comp, e, :, lanes] = (first[comp] + second[comp]) * SCALE


def convolve(head, lists, whole, every, per_energy):
    comps, energies, positions, rows, width = whole.shape
    total = lists.shape[0] // per_energy
    in_block = pl.BlockSpec(
        (comps, energies, pl.squeezed, rows, width), lambda p, h, l: (0, 0, p, 0, 0)
    )
    out_block = pl.BlockSpec(
        (comps, per_energy, pl.squeezed, rows, width), lambda p, h, l: (0, 0, p, 0, 0)
    )
    return pl.pallas_call(
        functools.partial(conv_kernel, per_energy, total),
        out_shape=jax.ShapeDtypeStruct((comps, per_energy, positions, rows, width), jnp.float32),
        grid_spec=pltpu.PrefetchScalarGridSpec(
            num_scalar_prefetch=2,
            grid=(positions,),
            in_specs=[in_block, in_block],
            out_specs=out_block,
        ),
        compiler_params=pltpu.CompilerParams(vmem_limit_bytes=48 * 1024 * 1024),
    )(head, lists, whole, every)


def per_device(green, screened, cell_map, shift_table, shift_count):
    cell_count = lax.axis_size("cell")
    per_energy = green.shape[1]
    per_cell = green.shape[2]
    width = green.shape[4]
    wanted = jnp.transpose(cell_map.reshape(cell_count, per_cell)).reshape(-1)
    outgoing = jnp.take(screened, wanted, axis=2)
    outgoing = outgoing.reshape(4, per_energy, per_cell, cell_count, screened.shape[3], width)
    arrived = lax.all_to_all(outgoing, "cell", split_axis=3, concat_axis=3, tiled=True)
    owned = arrived.reshape(4, per_energy, per_cell, green.shape[3], width)
    whole = lax.all_gather(green, "energy", axis=1, tiled=True)
    every = lax.all_gather(owned, "energy", axis=1, tiled=True)
    group = lax.axis_index("energy")
    head, lists = term_lists(shift_table, shift_count, group, per_energy)
    return convolve(head, lists, whole, every, per_energy)


def solution(mesh):
    placed = (
        P(None, "energy", "cell", None, None),
        P(None, "energy", None, "cell", None),
        P(),
        P(),
        P(),
    )
    return jax.shard_map(
        per_device,
        mesh=mesh,
        in_specs=placed,
        out_specs=P(None, "energy", "cell", None, None),
        check_vma=False,
    )
```

```python
import functools

import jax
import jax.numpy as jnp
from jax import lax
from jax.experimental import pallas as pl
from jax.experimental.pallas import tpu as pltpu
from jax.sharding import PartitionSpec as P

SCALE = 0.2
LANES = 128


def multiplicity(shift_table, shift_count, group, per_energy):
    groups, slot_count = shift_table.shape[1], shift_table.shape[2]
    table_row = shift_table[group]
    counts = shift_count[group]
    slot = lax.broadcasted_iota(jnp.int32, (groups, slot_count, 1), 1)
    offset = lax.broadcasted_iota(jnp.int32, (1, 1, per_energy), 2)
    hit = (slot < counts[:, None, None]) & (table_row[:, :, None] == offset)
    return jnp.sum(hit.astype(jnp.float32), axis=1).reshape(groups * per_energy)


def ring_conv_kernel(chips, mult_ref, w_hbm, g_hbm, o_ref, g_vmem, slots,
                     g_sem, local_sem, ring_send, ring_recv, pass_send, pass_recv):
    comps, per_energy, positions, rows, width = o_ref.shape
    me = lax.axis_index("energy")
    cell = lax.axis_index("cell")
    chip, core = me // 2, me % 2
    step_dir = 1 - 2 * core
    partner = me + step_dir
    ahead = 2 * ((chip + step_dir + chips) % chips) + core
    base = me * per_energy

    def origin(k):
        return 2 * ((chip - step_dir * k + chips) % chips) + core

    def handed_slot(k):
        return 2 * ((chip + step_dir * k + chips) % chips) + 1 - core

    def remote(src, slot, send, recv, k, target):
        return pltpu.make_async_remote_copy(
            src_ref=src, dst_ref=slots.at[slot],
            send_sem=send.at[k], recv_sem=recv.at[k],
            device_id=(target, cell), device_id_type=pl.DeviceIdType.MESH,
        )

    def ring_copy(k):
        slot = origin(k - 1)
        src = w_hbm if k == 1 else slots.at[slot]
        return remote(src, slot, ring_send, ring_recv, k, ahead)

    def pass_copy(k):
        slot = origin(k)
        src = w_hbm if k == 0 else slots.at[slot]
        return remote(src, slot, pass_send, pass_recv, k, partner)

    def arrival(k):
        slot = origin(k)
        return remote(slots.at[slot], slot, ring_send, ring_recv, k, ahead)

    def handed(k):
        slot = handed_slot(k)
        return remote(slots.at[slot], slot, pass_send, pass_recv, k, partner)

    def compute(source):
        @pl.when(source <= me)
        def _():
            def over_offset(j, carry):
                weight = mult_ref[source * per_energy + j]
                lag = base - source * per_energy - j
                for p in range(positions):
                    for chunk in range(width // LANES):
                        lanes = pl.ds(chunk * LANES, LANES)
                        wv = [slots[source, comp, j, p, :, lanes].astype(jnp.float32) * weight
                              for comp in range(comps)]

                        def over_energy(e, c2, p=p, lanes=lanes, wv=wv):
                            u = lag + e

                            @pl.when(u >= 0)
                            def _():
                                for kind in range(2):
                                    gr = g_vmem[2 * kind, u, p, :, lanes].astype(jnp.float32)
                                    gi = g_vmem[2 * kind + 1, u, p, :, lanes].astype(jnp.float32)
                                    wr, wi = wv[2 * kind], wv[2 * kind + 1]
                                    o_ref[2 * kind, e, p, :, lanes] -= gr * wi + gi * wr
                                    o_ref[2 * kind + 1, e, p, :, lanes] += gr * wr - gi * wi

                            return c2

                        lax.fori_loop(0, per_energy, over_energy, 0)
                return carry

            lax.fori_loop(0, per_energy, over_offset, 0)

    g_copy = pltpu.make_async_copy(g_hbm, g_vmem, g_sem)
    g_copy.start()
    local = pltpu.make_async_copy(w_hbm, slots.at[me], local_sem)
    local.start()
    sends = [ring_copy(1), pass_copy(0)]
    for copy in sends:
        copy.start()
    o_ref[...] = jnp.zeros(o_ref.shape, o_ref.dtype)
    g_copy.wait()
    local.wait()
    compute(me)
    for k in range(1, chips):
        arrival(k).wait_recv()
        onward = [pass_copy(k)]
        if k + 1 < chips:
            onward.append(ring_copy(k + 1))
        for copy in onward:
            copy.start()
        sends.extend(onward)
        compute(origin(k))
        handed(k - 1).wait_recv()
        compute(handed_slot(k - 1))
    handed(chips - 1).wait_recv()
    compute(handed_slot(chips - 1))
    for copy in sends:
        copy.wait_send()
    o_ref[...] = o_ref[...] * SCALE


def ring_convolve(mult, owned, whole):
    groups = lax.axis_size("energy")
    chips = groups // 2
    return pl.pallas_call(
        functools.partial(ring_conv_kernel, chips),
        out_shape=jax.ShapeDtypeStruct(owned.shape, jnp.float32),
        in_specs=[
            pl.BlockSpec(memory_space=pltpu.SMEM),
            pl.BlockSpec(memory_space=pl.ANY),
            pl.BlockSpec(memory_space=pl.ANY),
        ],
        out_specs=pl.BlockSpec(memory_space=pltpu.VMEM),
        scratch_shapes=[
            pltpu.VMEM(whole.shape, whole.dtype),
            pltpu.VMEM((groups,) + owned.shape, owned.dtype),
            pltpu.SemaphoreType.DMA(()),
            pltpu.SemaphoreType.DMA(()),
            pltpu.SemaphoreType.DMA((chips,)),
            pltpu.SemaphoreType.DMA((chips,)),
            pltpu.SemaphoreType.DMA((chips,)),
            pltpu.SemaphoreType.DMA((chips,)),
        ],
        compiler_params=pltpu.CompilerParams(
            has_side_effects=True, vmem_limit_bytes=48 * 1024 * 1024
        ),
    )(mult, owned, whole)


def per_device(green, screened, cell_map, shift_table, shift_count):
    cell_count = lax.axis_size("cell")
    per_energy = green.shape[1]
    per_cell = green.shape[2]
    width = green.shape[4]
    wanted = jnp.transpose(cell_map.reshape(cell_count, per_cell)).reshape(-1)
    outgoing = jnp.take(screened, wanted, axis=2)
    outgoing = outgoing.reshape(4, per_energy, per_cell, cell_count, screened.shape[3], width)
    arrived = lax.all_to_all(outgoing, "cell", split_axis=3, concat_axis=3, tiled=True)
    owned = arrived.reshape(4, per_energy, per_cell, green.shape[3], width)
    whole = lax.all_gather(green, "energy", axis=1, tiled=True)
    group = lax.axis_index("energy")
    mult = multiplicity(shift_table, shift_count, group, per_energy)
    return ring_convolve(mult, owned, whole)


def solution(mesh):
    placed = (
        P(None, "energy", "cell", None, None),
        P(None, "energy", None, "cell", None),
        P(),
        P(),
        P(),
    )
    return jax.shard_map(
        per_device,
        mesh=mesh,
        in_specs=placed,
        out_specs=P(None, "energy", "cell", None, None),
        check_vma=False,
    )
```

```python
import functools

import jax
import jax.numpy as jnp
from jax import lax
from jax.experimental import pallas as pl
from jax.experimental.pallas import tpu as pltpu
from jax.sharding import PartitionSpec as P

SCALE = 0.2
LANES = 128


def slot_tables(shift_table, shift_count, group):
    groups, slot_count = shift_table.shape[1], shift_table.shape[2]
    slot = lax.broadcasted_iota(jnp.int32, (groups, slot_count), 1)
    live = (slot < shift_count[group][:, None]).astype(jnp.float32)
    return shift_table[group].reshape(-1), live.reshape(-1)


def ring_conv_kernel(chips, slot_count, shift_ref, live_ref, w_hbm, g_hbm, o_ref, g_vmem, *scratch):
    own_buf = scratch[0]
    ring_bufs = (None,) + tuple(scratch[1:chips])
    hand_bufs = tuple(scratch[chips:2 * chips])
    g_sem, local_sem, ring_send, ring_recv, pass_send, pass_recv = scratch[2 * chips:]
    comps, per_energy, positions, rows, width = o_ref.shape
    me = lax.axis_index("energy")
    cell = lax.axis_index("cell")
    chip, core = me // 2, me % 2
    step_dir = 1 - 2 * core
    partner = me + step_dir
    ahead = 2 * ((chip + step_dir + chips) % chips) + core
    base = me * per_energy

    def origin(k):
        return 2 * ((chip - step_dir * k + chips) % chips) + core

    def handed_group(k):
        return 2 * ((chip + step_dir * k + chips) % chips) + 1 - core

    def remote(src, dst, send, recv, k, target):
        return pltpu.make_async_remote_copy(
            src_ref=src, dst_ref=dst, send_sem=send.at[k], recv_sem=recv.at[k],
            device_id=(target, cell), device_id_type=pl.DeviceIdType.MESH,
        )

    def ring_copy(k):
        src = w_hbm if k == 1 else ring_bufs[k - 1]
        return remote(src, ring_bufs[k], ring_send, ring_recv, k, ahead)

    def pass_copy(k):
        src = w_hbm if k == 0 else ring_bufs[k]
        return remote(src, hand_bufs[k], pass_send, pass_recv, k, partner)

    def arrival(k):
        return remote(ring_bufs[k], ring_bufs[k], ring_send, ring_recv, k, ahead)

    def handed(k):
        return remote(hand_bufs[k], hand_bufs[k], pass_send, pass_recv, k, partner)

    def compute(source, buf, masked):
        lag = base - source * per_energy

        def run():
            for p in range(positions):
                for chunk in range(width // LANES):
                    lanes = pl.ds(chunk * LANES, LANES)

                    def over_energy(e, carry, p=p, lanes=lanes):
                        acc = [jnp.zeros((rows, LANES), jnp.float32)] * comps
                        for c in range(slot_count):
                            j = shift_ref[source * slot_count + c]
                            weight = live_ref[source * slot_count + c]
                            u = lag + e - j
                            if masked:
                                weight = jnp.where(u >= 0, weight, 0.0)
                                u = jnp.maximum(u, 0)
                            for kind in range(2):
                                gr = g_vmem[2 * kind, u, p, :, lanes].astype(jnp.float32)
                                gi = g_vmem[2 * kind + 1, u, p, :, lanes].astype(jnp.float32)
                                wr = buf[2 * kind, j, p, :, lanes].astype(jnp.float32) * weight
                                wi = buf[2 * kind + 1, j, p, :, lanes].astype(jnp.float32) * weight
                                acc[2 * kind] = acc[2 * kind] - (gr * wi + gi * wr)
                                acc[2 * kind + 1] = acc[2 * kind + 1] + (gr * wr - gi * wi)
                        for comp in range(comps):
                            o_ref[comp, e, p, :, lanes] += acc[comp]
                        return carry

                    lax.fori_loop(0, per_energy, over_energy, 0)

        if masked:
            run()
        else:
            pl.when(source < me)(run)

    g_copy = pltpu.make_async_copy(g_hbm, g_vmem, g_sem)
    g_copy.start()
    local = pltpu.make_async_copy(w_hbm, own_buf, local_sem)
    local.start()
    sends = [ring_copy(1), pass_copy(0)]
    for copy in sends:
        copy.start()
    o_ref[...] = jnp.zeros(o_ref.shape, o_ref.dtype)
    g_copy.wait()
    local.wait()
    compute(me, own_buf, True)
    for k in range(1, chips):
        arrival(k).wait_recv()
        onward = [pass_copy(k)]
        if k + 1 < chips:
            onward.append(ring_copy(k + 1))
        for copy in onward:
            copy.start()
        sends.extend(onward)
        compute(origin(k), ring_bufs[k], False)
        handed(k - 1).wait_recv()
        compute(handed_group(k - 1), hand_bufs[k - 1], False)
    handed(chips - 1).wait_recv()
    compute(handed_group(chips - 1), hand_bufs[chips - 1], False)
    for copy in sends:
        copy.wait_send()
    o_ref[...] = o_ref[...] * SCALE


def ring_convolve(shifts, lives, owned, whole, slot_count):
    groups = lax.axis_size("energy")
    chips = groups // 2
    block = pltpu.VMEM(owned.shape, owned.dtype)
    return pl.pallas_call(
        functools.partial(ring_conv_kernel, chips, slot_count),
        out_shape=jax.ShapeDtypeStruct(owned.shape, jnp.float32),
        in_specs=[
            pl.BlockSpec(memory_space=pltpu.SMEM),
            pl.BlockSpec(memory_space=pltpu.SMEM),
            pl.BlockSpec(memory_space=pl.ANY),
            pl.BlockSpec(memory_space=pl.ANY),
        ],
        out_specs=pl.BlockSpec(memory_space=pltpu.VMEM),
        scratch_shapes=[pltpu.VMEM(whole.shape, whole.dtype)]
        + [block] * (2 * chips)
        + [
            pltpu.SemaphoreType.DMA(()),
            pltpu.SemaphoreType.DMA(()),
            pltpu.SemaphoreType.DMA((chips,)),
            pltpu.SemaphoreType.DMA((chips,)),
            pltpu.SemaphoreType.DMA((chips,)),
            pltpu.SemaphoreType.DMA((chips,)),
        ],
        compiler_params=pltpu.CompilerParams(
            has_side_effects=True, vmem_limit_bytes=48 * 1024 * 1024
        ),
    )(shifts, lives, owned, whole)


def per_device(green, screened, cell_map, shift_table, shift_count):
    cell_count = lax.axis_size("cell")
    per_energy = green.shape[1]
    per_cell = green.shape[2]
    width = green.shape[4]
    wanted = jnp.transpose(cell_map.reshape(cell_count, per_cell)).reshape(-1)
    outgoing = jnp.take(screened, wanted, axis=2)
    outgoing = outgoing.reshape(4, per_energy, per_cell, cell_count, screened.shape[3], width)
    arrived = lax.all_to_all(outgoing, "cell", split_axis=3, concat_axis=3, tiled=True)
    owned = arrived.reshape(4, per_energy, per_cell, green.shape[3], width)
    whole = lax.all_gather(green, "energy", axis=1, tiled=True)
    group = lax.axis_index("energy")
    shifts, lives = slot_tables(shift_table, shift_count, group)
    return ring_convolve(shifts, lives, owned, whole, shift_table.shape[2])


def solution(mesh):
    placed = (
        P(None, "energy", "cell", None, None),
        P(None, "energy", None, "cell", None),
        P(),
        P(),
        P(),
    )
    return jax.shard_map(
        per_device,
        mesh=mesh,
        in_specs=placed,
        out_specs=P(None, "energy", "cell", None, None),
        check_vma=False,
    )
```

```python
import functools

import jax
import jax.numpy as jnp
from jax import lax
from jax.experimental import pallas as pl
from jax.experimental.pallas import tpu as pltpu
from jax.sharding import PartitionSpec as P

SCALE = 0.2
LANES = 128


def slot_tables(shift_table, shift_count, group):
    groups, slot_count = shift_table.shape[1], shift_table.shape[2]
    slot = lax.broadcasted_iota(jnp.int32, (groups, slot_count), 1)
    live = (slot < shift_count[group][:, None]).astype(jnp.float32)
    return shift_table[group].reshape(-1), live.reshape(-1)


def ring_conv_kernel(chips, slot_count, shift_ref, live_ref, w_hbm, g_hbm, o_ref, g_vmem, *scratch):
    halves = 2
    count = 2 * chips
    bufs = [scratch[h * count:(h + 1) * count] for h in range(halves)]
    own_bufs = [b[0] for b in bufs]
    ring_bufs = [(None,) + tuple(b[1:chips]) for b in bufs]
    hand_bufs = [tuple(b[chips:count]) for b in bufs]
    g_sem, local_sem, ring_send, ring_recv, pass_send, pass_recv = scratch[halves * count:]
    comps, per_energy, positions, rows, width = o_ref.shape
    me = lax.axis_index("energy")
    cell = lax.axis_index("cell")
    chip, core = me // 2, me % 2
    step_dir = 1 - 2 * core
    partner = me + step_dir
    ahead = 2 * ((chip + step_dir + chips) % chips) + core
    base = me * per_energy

    def origin(k):
        return 2 * ((chip - step_dir * k + chips) % chips) + core

    def handed_group(k):
        return 2 * ((chip + step_dir * k + chips) % chips) + 1 - core

    def own_half(h):
        return w_hbm.at[pl.ds(2 * h, 2)]

    def remote(src, dst, send, recv, k, h, target):
        return pltpu.make_async_remote_copy(
            src_ref=src, dst_ref=dst, send_sem=send.at[k, h], recv_sem=recv.at[k, h],
            device_id=(target, cell), device_id_type=pl.DeviceIdType.MESH,
        )

    def ring_copy(k, h):
        src = own_half(h) if k == 1 else ring_bufs[h][k - 1]
        return remote(src, ring_bufs[h][k], ring_send, ring_recv, k, h, ahead)

    def pass_copy(k, h):
        src = own_half(h) if k == 0 else ring_bufs[h][k]
        return remote(src, hand_bufs[h][k], pass_send, pass_recv, k, h, partner)

    def arrival(k, h):
        return remote(ring_bufs[h][k], ring_bufs[h][k], ring_send, ring_recv, k, h, ahead)

    def handed(k, h):
        return remote(hand_bufs[h][k], hand_bufs[h][k], pass_send, pass_recv, k, h, partner)

    def compute(source, buf, kind, masked):
        lag = base - source * per_energy

        def run():
            for p in range(positions):
                for chunk in range(width // LANES):
                    lanes = pl.ds(chunk * LANES, LANES)

                    def over_energy(e, carry, p=p, lanes=lanes):
                        real = jnp.zeros((rows, LANES), jnp.float32)
                        imag = jnp.zeros((rows, LANES), jnp.float32)
                        for c in range(slot_count):
                            j = shift_ref[source * slot_count + c]
                            weight = live_ref[source * slot_count + c]
                            u = lag + e - j
                            if masked:
                                weight = jnp.where(u >= 0, weight, 0.0)
                                u = jnp.maximum(u, 0)
                            gr = g_vmem[2 * kind, u, p, :, lanes].astype(jnp.float32)
                            gi = g_vmem[2 * kind + 1, u, p, :, lanes].astype(jnp.float32)
                            wr = buf[0, j, p, :, lanes].astype(jnp.float32) * weight
                            wi = buf[1, j, p, :, lanes].astype(jnp.float32) * weight
                            real = real - (gr * wi + gi * wr)
                            imag = imag + (gr * wr - gi * wi)
                        o_ref[2 * kind, e, p, :, lanes] += real
                        o_ref[2 * kind + 1, e, p, :, lanes] += imag
                        return carry

                    lax.fori_loop(0, per_energy, over_energy, 0)

        if masked:
            run()
        else:
            pl.when(source < me)(run)

    g_copy = pltpu.make_async_copy(g_hbm, g_vmem, g_sem)
    g_copy.start()
    locals_ = [pltpu.make_async_copy(own_half(h), own_bufs[h], local_sem.at[h]) for h in range(halves)]
    for copy in locals_:
        copy.start()
    sends = [ring_copy(1, h) for h in range(halves)] + [pass_copy(0, h) for h in range(halves)]
    for copy in sends:
        copy.start()
    o_ref[...] = jnp.zeros(o_ref.shape, o_ref.dtype)
    g_copy.wait()
    for h in range(halves):
        locals_[h].wait()
        compute(me, own_bufs[h], h, True)
    for k in range(1, chips):
        for h in range(halves):
            arrival(k, h).wait_recv()
            onward = [pass_copy(k, h)]
            if k + 1 < chips:
                onward.append(ring_copy(k + 1, h))
            for copy in onward:
                copy.start()
            sends.extend(onward)
            compute(origin(k), ring_bufs[h][k], h, False)
        for h in range(halves):
            handed(k - 1, h).wait_recv()
            compute(handed_group(k - 1), hand_bufs[h][k - 1], h, False)
    for h in range(halves):
        handed(chips - 1, h).wait_recv()
        compute(handed_group(chips - 1), hand_bufs[h][chips - 1], h, False)
    for copy in sends:
        copy.wait_send()
    o_ref[...] = o_ref[...] * SCALE


def ring_convolve(shifts, lives, owned, whole, slot_count):
    groups = lax.axis_size("energy")
    chips = groups // 2
    half = pltpu.VMEM((owned.shape[0] // 2,) + owned.shape[1:], owned.dtype)
    return pl.pallas_call(
        functools.partial(ring_conv_kernel, chips, slot_count),
        out_shape=jax.ShapeDtypeStruct(owned.shape, jnp.float32),
        in_specs=[
            pl.BlockSpec(memory_space=pltpu.SMEM),
            pl.BlockSpec(memory_space=pltpu.SMEM),
            pl.BlockSpec(memory_space=pl.ANY),
            pl.BlockSpec(memory_space=pl.ANY),
        ],
        out_specs=pl.BlockSpec(memory_space=pltpu.VMEM),
        scratch_shapes=[pltpu.VMEM(whole.shape, whole.dtype)]
        + [half] * (4 * chips)
        + [
            pltpu.SemaphoreType.DMA(()),
            pltpu.SemaphoreType.DMA((2,)),
            pltpu.SemaphoreType.DMA((chips, 2)),
            pltpu.SemaphoreType.DMA((chips, 2)),
            pltpu.SemaphoreType.DMA((chips, 2)),
            pltpu.SemaphoreType.DMA((chips, 2)),
        ],
        compiler_params=pltpu.CompilerParams(
            has_side_effects=True, vmem_limit_bytes=48 * 1024 * 1024
        ),
    )(shifts, lives, owned, whole)


def per_device(green, screened, cell_map, shift_table, shift_count):
    cell_count = lax.axis_size("cell")
    per_energy = green.shape[1]
    per_cell = green.shape[2]
    width = green.shape[4]
    wanted = jnp.transpose(cell_map.reshape(cell_count, per_cell)).reshape(-1)
    outgoing = jnp.take(screened, wanted, axis=2)
    outgoing = outgoing.reshape(4, per_energy, per_cell, cell_count, screened.shape[3], width)
    arrived = lax.all_to_all(outgoing, "cell", split_axis=3, concat_axis=3, tiled=True)
    owned = arrived.reshape(4, per_energy, per_cell, green.shape[3], width)
    whole = lax.all_gather(green, "energy", axis=1, tiled=True)
    group = lax.axis_index("energy")
    shifts, lives = slot_tables(shift_table, shift_count, group)
    return ring_convolve(shifts, lives, owned, whole, shift_table.shape[2])


def solution(mesh):
    placed = (
        P(None, "energy", "cell", None, None),
        P(None, "energy", None, "cell", None),
        P(),
        P(),
        P(),
    )
    return jax.shard_map(
        per_device,
        mesh=mesh,
        in_specs=placed,
        out_specs=P(None, "energy", "cell", None, None),
        check_vma=False,
    )
```

```python
import functools

import jax
import jax.numpy as jnp
from jax import lax
from jax.experimental import pallas as pl
from jax.experimental.pallas import tpu as pltpu
from jax.sharding import PartitionSpec as P

SCALE = 0.2
LANES = 128
PIECE = 256


def slot_tables(shift_table, shift_count, group):
    groups, slot_count = shift_table.shape[1], shift_table.shape[2]
    slot = lax.broadcasted_iota(jnp.int32, (groups, slot_count), 1)
    live = (slot < shift_count[group][:, None]).astype(jnp.float32)
    return shift_table[group].reshape(-1), live.reshape(-1)


def ring_conv_kernel(chips, slot_count, shift_ref, live_ref, w_hbm, g_hbm, o_ref, g_vmem, *scratch):
    lane_parts = o_ref.shape[4] // PIECE
    halves = 2 * lane_parts
    count = 2 * chips
    bufs = [scratch[h * count:(h + 1) * count] for h in range(halves)]
    own_bufs = [b[0] for b in bufs]
    ring_bufs = [(None,) + tuple(b[1:chips]) for b in bufs]
    hand_bufs = [tuple(b[chips:count]) for b in bufs]
    g_sem, local_sem, ring_send, ring_recv, pass_send, pass_recv = scratch[halves * count:]
    comps, per_energy, positions, rows, width = o_ref.shape
    me = lax.axis_index("energy")
    cell = lax.axis_index("cell")
    chip, core = me // 2, me % 2
    step_dir = 1 - 2 * core
    partner = me + step_dir
    ahead = 2 * ((chip + step_dir + chips) % chips) + core
    base = me * per_energy

    def origin(k):
        return 2 * ((chip - step_dir * k + chips) % chips) + core

    def handed_group(k):
        return 2 * ((chip + step_dir * k + chips) % chips) + 1 - core

    def own_half(h):
        kind, part = h // lane_parts, h % lane_parts
        return w_hbm.at[pl.ds(2 * kind, 2), :, :, :, pl.ds(part * PIECE, PIECE)]

    def remote(src, dst, send, recv, k, h, target):
        return pltpu.make_async_remote_copy(
            src_ref=src, dst_ref=dst, send_sem=send.at[k, h], recv_sem=recv.at[k, h],
            device_id=(target, cell), device_id_type=pl.DeviceIdType.MESH,
        )

    def ring_copy(k, h):
        src = own_half(h) if k == 1 else ring_bufs[h][k - 1]
        return remote(src, ring_bufs[h][k], ring_send, ring_recv, k, h, ahead)

    def pass_copy(k, h):
        src = own_half(h) if k == 0 else ring_bufs[h][k]
        return remote(src, hand_bufs[h][k], pass_send, pass_recv, k, h, partner)

    def arrival(k, h):
        return remote(ring_bufs[h][k], ring_bufs[h][k], ring_send, ring_recv, k, h, ahead)

    def handed(k, h):
        return remote(hand_bufs[h][k], hand_bufs[h][k], pass_send, pass_recv, k, h, partner)

    def compute(source, buf, h, masked):
        lag = base - source * per_energy
        kind, part = h // lane_parts, h % lane_parts

        def run():
            for p in range(positions):
                for chunk in range(PIECE // LANES):
                    local = pl.ds(chunk * LANES, LANES)
                    lanes = pl.ds(part * PIECE + chunk * LANES, LANES)

                    def over_energy(e, carry, p=p, lanes=lanes, local=local):
                        real = jnp.zeros((rows, LANES), jnp.float32)
                        imag = jnp.zeros((rows, LANES), jnp.float32)
                        for c in range(slot_count):
                            j = shift_ref[source * slot_count + c]
                            weight = live_ref[source * slot_count + c]
                            u = lag + e - j
                            if masked:
                                weight = jnp.where(u >= 0, weight, 0.0)
                                u = jnp.maximum(u, 0)
                            gr = g_vmem[2 * kind, u, p, :, lanes].astype(jnp.float32)
                            gi = g_vmem[2 * kind + 1, u, p, :, lanes].astype(jnp.float32)
                            wr = buf[0, j, p, :, local].astype(jnp.float32) * weight
                            wi = buf[1, j, p, :, local].astype(jnp.float32) * weight
                            real = real - (gr * wi + gi * wr)
                            imag = imag + (gr * wr - gi * wi)
                        o_ref[2 * kind, e, p, :, lanes] += real
                        o_ref[2 * kind + 1, e, p, :, lanes] += imag
                        return carry

                    lax.fori_loop(0, per_energy, over_energy, 0)

        if masked:
            run()
        else:
            pl.when(source < me)(run)

    g_copy = pltpu.make_async_copy(g_hbm, g_vmem, g_sem)
    g_copy.start()
    locals_ = [pltpu.make_async_copy(own_half(h), own_bufs[h], local_sem.at[h]) for h in range(halves)]
    for copy in locals_:
        copy.start()
    sends = [ring_copy(1, h) for h in range(halves)] + [pass_copy(0, h) for h in range(halves)]
    for copy in sends:
        copy.start()
    o_ref[...] = jnp.zeros(o_ref.shape, o_ref.dtype)
    g_copy.wait()
    for h in range(halves):
        locals_[h].wait()
        compute(me, own_bufs[h], h, True)
    for k in range(1, chips):
        for h in range(halves):
            arrival(k, h).wait_recv()
            onward = [pass_copy(k, h)]
            if k + 1 < chips:
                onward.append(ring_copy(k + 1, h))
            for copy in onward:
                copy.start()
            sends.extend(onward)
            compute(origin(k), ring_bufs[h][k], h, False)
        for h in range(halves):
            handed(k - 1, h).wait_recv()
            compute(handed_group(k - 1), hand_bufs[h][k - 1], h, False)
    for h in range(halves):
        handed(chips - 1, h).wait_recv()
        compute(handed_group(chips - 1), hand_bufs[h][chips - 1], h, False)
    for copy in sends:
        copy.wait_send()
    o_ref[...] = o_ref[...] * SCALE


def ring_convolve(shifts, lives, owned, whole, slot_count):
    groups = lax.axis_size("energy")
    chips = groups // 2
    pieces = 2 * (owned.shape[4] // PIECE)
    half = pltpu.VMEM((owned.shape[0] // 2,) + owned.shape[1:4] + (PIECE,), owned.dtype)
    return pl.pallas_call(
        functools.partial(ring_conv_kernel, chips, slot_count),
        out_shape=jax.ShapeDtypeStruct(owned.shape, jnp.float32),
        in_specs=[
            pl.BlockSpec(memory_space=pltpu.SMEM),
            pl.BlockSpec(memory_space=pltpu.SMEM),
            pl.BlockSpec(memory_space=pl.ANY),
            pl.BlockSpec(memory_space=pl.ANY),
        ],
        out_specs=pl.BlockSpec(memory_space=pltpu.VMEM),
        scratch_shapes=[pltpu.VMEM(whole.shape, whole.dtype)]
        + [half] * (2 * chips * pieces)
        + [
            pltpu.SemaphoreType.DMA(()),
            pltpu.SemaphoreType.DMA((pieces,)),
            pltpu.SemaphoreType.DMA((chips, pieces)),
            pltpu.SemaphoreType.DMA((chips, pieces)),
            pltpu.SemaphoreType.DMA((chips, pieces)),
            pltpu.SemaphoreType.DMA((chips, pieces)),
        ],
        compiler_params=pltpu.CompilerParams(
            has_side_effects=True, vmem_limit_bytes=48 * 1024 * 1024
        ),
    )(shifts, lives, owned, whole)


def per_device(green, screened, cell_map, shift_table, shift_count):
    cell_count = lax.axis_size("cell")
    per_energy = green.shape[1]
    per_cell = green.shape[2]
    width = green.shape[4]
    wanted = jnp.transpose(cell_map.reshape(cell_count, per_cell)).reshape(-1)
    outgoing = jnp.take(screened, wanted, axis=2)
    outgoing = outgoing.reshape(4, per_energy, per_cell, cell_count, screened.shape[3], width)
    arrived = lax.all_to_all(outgoing, "cell", split_axis=3, concat_axis=3, tiled=True)
    owned = arrived.reshape(4, per_energy, per_cell, green.shape[3], width)
    whole = lax.all_gather(green, "energy", axis=1, tiled=True)
    group = lax.axis_index("energy")
    shifts, lives = slot_tables(shift_table, shift_count, group)
    return ring_convolve(shifts, lives, owned, whole, shift_table.shape[2])


def solution(mesh):
    placed = (
        P(None, "energy", "cell", None, None),
        P(None, "energy", None, "cell", None),
        P(),
        P(),
        P(),
    )
    return jax.shard_map(
        per_device,
        mesh=mesh,
        in_specs=placed,
        out_specs=P(None, "energy", "cell", None, None),
        check_vma=False,
    )
```

```python
import functools

import jax
import jax.numpy as jnp
from jax import lax
from jax.experimental import pallas as pl
from jax.experimental.pallas import tpu as pltpu
from jax.sharding import PartitionSpec as P

SCALE = 0.2
LANES = 128


def slot_tables(shift_table, shift_count, group):
    groups, slot_count = shift_table.shape[1], shift_table.shape[2]
    slot = lax.broadcasted_iota(jnp.int32, (groups, slot_count), 1)
    live = (slot < shift_count[group][:, None]).astype(jnp.float32)
    return shift_table[group].reshape(-1), live.reshape(-1)


def ring_conv_kernel(chips, slot_count, shift_ref, live_ref, w_hbm, g_hbm, o_ref, g_vmem, *scratch):
    halves = 2
    count = 2 * chips
    bufs = [scratch[h * count:(h + 1) * count] for h in range(halves)]
    own_bufs = [b[0] for b in bufs]
    ring_bufs = [(None,) + tuple(b[1:chips]) for b in bufs]
    hand_bufs = [tuple(b[chips:count]) for b in bufs]
    g_sem, local_sem, ring_send, ring_recv, pass_send, pass_recv = scratch[halves * count:]
    comps, per_energy, positions, rows, width = o_ref.shape
    me = lax.axis_index("energy")
    cell = lax.axis_index("cell")
    chip, core = me // 2, me % 2
    step_dir = 1 - 2 * core
    partner = me + step_dir
    ahead = 2 * ((chip + step_dir + chips) % chips) + core
    base = me * per_energy

    def origin(k):
        return 2 * ((chip - step_dir * k + chips) % chips) + core

    def handed_group(k):
        return 2 * ((chip + step_dir * k + chips) % chips) + 1 - core

    def own_half(h):
        return w_hbm.at[pl.ds(2 * h, 2)]

    def remote(src, dst, send, recv, k, h, target):
        return pltpu.make_async_remote_copy(
            src_ref=src, dst_ref=dst, send_sem=send.at[k, h], recv_sem=recv.at[k, h],
            device_id=(target, cell), device_id_type=pl.DeviceIdType.MESH,
        )

    def ring_copy(k, h):
        src = own_half(h) if k == 1 else ring_bufs[h][k - 1]
        return remote(src, ring_bufs[h][k], ring_send, ring_recv, k, h, ahead)

    def pass_copy(k, h):
        src = own_half(h) if k == 0 else ring_bufs[h][k]
        return remote(src, hand_bufs[h][k], pass_send, pass_recv, k, h, partner)

    def arrival(k, h):
        return remote(ring_bufs[h][k], ring_bufs[h][k], ring_send, ring_recv, k, h, ahead)

    def handed(k, h):
        return remote(hand_bufs[h][k], hand_bufs[h][k], pass_send, pass_recv, k, h, partner)

    def compute(source, buf, kind, masked):
        lag = base - source * per_energy

        def run():
            for p in range(positions):
                for chunk in range(width // LANES):
                    lanes = pl.ds(chunk * LANES, LANES)

                    def over_energy(e, carry, p=p, lanes=lanes):
                        real = jnp.zeros((rows, LANES), jnp.float32)
                        imag = jnp.zeros((rows, LANES), jnp.float32)
                        for c in range(slot_count):
                            j = shift_ref[source * slot_count + c]
                            weight = live_ref[source * slot_count + c]
                            u = lag + e - j
                            if masked:
                                weight = jnp.where(u >= 0, weight, 0.0)
                                u = jnp.maximum(u, 0)
                            gr = g_vmem[2 * kind, u, p, :, lanes].astype(jnp.float32)
                            gi = g_vmem[2 * kind + 1, u, p, :, lanes].astype(jnp.float32)
                            wr = buf[0, j, p, :, lanes].astype(jnp.float32) * weight
                            wi = buf[1, j, p, :, lanes].astype(jnp.float32) * weight
                            real = real - (gr * wi + gi * wr)
                            imag = imag + (gr * wr - gi * wi)
                        o_ref[2 * kind, e, p, :, lanes] += real
                        o_ref[2 * kind + 1, e, p, :, lanes] += imag
                        return carry

                    lax.fori_loop(0, per_energy, over_energy, 0)

        if masked:
            run()
        else:
            pl.when(source < me)(run)

    g_copy = pltpu.make_async_copy(g_hbm, g_vmem, g_sem)
    g_copy.start()
    locals_ = [pltpu.make_async_copy(own_half(h), own_bufs[h], local_sem.at[h]) for h in range(halves)]
    for copy in locals_:
        copy.start()
    sends = [ring_copy(1, h) for h in range(halves)] + [pass_copy(0, h) for h in range(halves)]
    for copy in sends:
        copy.start()
    o_ref[...] = jnp.zeros(o_ref.shape, o_ref.dtype)
    g_copy.wait()
    for h in range(halves):
        locals_[h].wait()
        compute(me, own_bufs[h], h, True)
    for k in range(1, chips):
        for h in range(halves):
            arrival(k, h).wait_recv()
            onward = [pass_copy(k, h)]
            if k + 1 < chips:
                onward.append(ring_copy(k + 1, h))
            for copy in onward:
                copy.start()
            sends.extend(onward)
            compute(origin(k), ring_bufs[h][k], h, False)
        for h in range(halves):
            handed(k - 1, h).wait_recv()
            compute(handed_group(k - 1), hand_bufs[h][k - 1], h, False)
    for h in range(halves):
        handed(chips - 1, h).wait_recv()
        compute(handed_group(chips - 1), hand_bufs[h][chips - 1], h, False)
    for copy in sends:
        copy.wait_send()
    o_ref[...] = o_ref[...] * SCALE


def ring_convolve(shifts, lives, owned, whole, slot_count):
    groups = lax.axis_size("energy")
    chips = groups // 2
    half = pltpu.VMEM((owned.shape[0] // 2,) + owned.shape[1:], owned.dtype)
    return pl.pallas_call(
        functools.partial(ring_conv_kernel, chips, slot_count),
        out_shape=jax.ShapeDtypeStruct(owned.shape, jnp.float32),
        in_specs=[
            pl.BlockSpec(memory_space=pltpu.SMEM),
            pl.BlockSpec(memory_space=pltpu.SMEM),
            pl.BlockSpec(memory_space=pl.ANY),
            pl.BlockSpec(memory_space=pl.ANY),
        ],
        out_specs=pl.BlockSpec(memory_space=pltpu.VMEM),
        scratch_shapes=[pltpu.VMEM(whole.shape, whole.dtype)]
        + [half] * (4 * chips)
        + [
            pltpu.SemaphoreType.DMA(()),
            pltpu.SemaphoreType.DMA((2,)),
            pltpu.SemaphoreType.DMA((chips, 2)),
            pltpu.SemaphoreType.DMA((chips, 2)),
            pltpu.SemaphoreType.DMA((chips, 2)),
            pltpu.SemaphoreType.DMA((chips, 2)),
        ],
        compiler_params=pltpu.CompilerParams(
            has_side_effects=True, vmem_limit_bytes=48 * 1024 * 1024
        ),
    )(shifts, lives, owned, whole)


def gather_kernel(chips, x_hbm, out_ref, local_sem, ring_send, ring_recv, pass_send, pass_recv):
    halves = 2
    per_energy = x_hbm.shape[1]
    me = lax.axis_index("energy")
    cell = lax.axis_index("cell")
    chip, core = me // 2, me % 2
    step_dir = 1 - 2 * core
    partner = me + step_dir
    ahead = 2 * ((chip + step_dir + chips) % chips) + core

    def origin(k):
        return 2 * ((chip - step_dir * k + chips) % chips) + core

    def handed_group(k):
        return 2 * ((chip + step_dir * k + chips) % chips) + 1 - core

    def place(group, h):
        return out_ref.at[pl.ds(2 * h, 2), pl.ds(group * per_energy, per_energy)]

    def own_half(h):
        return x_hbm.at[pl.ds(2 * h, 2)]

    def remote(src, dst, send, recv, k, h, target):
        return pltpu.make_async_remote_copy(
            src_ref=src, dst_ref=dst, send_sem=send.at[k, h], recv_sem=recv.at[k, h],
            device_id=(target, cell), device_id_type=pl.DeviceIdType.MESH,
        )

    def ring_copy(k, h):
        src = own_half(h) if k == 1 else place(origin(k - 1), h)
        return remote(src, place(origin(k - 1), h), ring_send, ring_recv, k, h, ahead)

    def pass_copy(k, h):
        src = own_half(h) if k == 0 else place(origin(k), h)
        return remote(src, place(origin(k), h), pass_send, pass_recv, k, h, partner)

    def arrival(k, h):
        return remote(place(origin(k), h), place(origin(k), h), ring_send, ring_recv, k, h, ahead)

    def handed(k, h):
        slot = place(handed_group(k), h)
        return remote(slot, slot, pass_send, pass_recv, k, h, partner)

    locals_ = [pltpu.make_async_copy(own_half(h), place(me, h), local_sem.at[h]) for h in range(halves)]
    for copy in locals_:
        copy.start()
    sends = [ring_copy(1, h) for h in range(halves)] + [pass_copy(0, h) for h in range(halves)]
    for copy in sends:
        copy.start()
    for k in range(1, chips):
        for h in range(halves):
            arrival(k, h).wait_recv()
            onward = [pass_copy(k, h)]
            if k + 1 < chips:
                onward.append(ring_copy(k + 1, h))
            for copy in onward:
                copy.start()
            sends.extend(onward)
    for k in range(chips):
        for h in range(halves):
            handed(k, h).wait_recv()
    for copy in sends:
        copy.wait_send()
    for copy in locals_:
        copy.wait()


def ring_gather(block):
    groups = lax.axis_size("energy")
    chips = groups // 2
    shape = (block.shape[0], groups * block.shape[1]) + block.shape[2:]
    return pl.pallas_call(
        functools.partial(gather_kernel, chips),
        out_shape=jax.ShapeDtypeStruct(shape, block.dtype),
        in_specs=[pl.BlockSpec(memory_space=pl.ANY)],
        out_specs=pl.BlockSpec(memory_space=pl.ANY),
        scratch_shapes=[
            pltpu.SemaphoreType.DMA((2,)),
            pltpu.SemaphoreType.DMA((chips, 2)),
            pltpu.SemaphoreType.DMA((chips, 2)),
            pltpu.SemaphoreType.DMA((chips, 2)),
            pltpu.SemaphoreType.DMA((chips, 2)),
        ],
        compiler_params=pltpu.CompilerParams(has_side_effects=True),
    )(block)


def per_device(green, screened, cell_map, shift_table, shift_count):
    cell_count = lax.axis_size("cell")
    per_energy = green.shape[1]
    per_cell = green.shape[2]
    width = green.shape[4]
    wanted = jnp.transpose(cell_map.reshape(cell_count, per_cell)).reshape(-1)
    outgoing = jnp.take(screened, wanted, axis=2)
    outgoing = outgoing.reshape(4, per_energy, per_cell, cell_count, screened.shape[3], width)
    arrived = lax.all_to_all(outgoing, "cell", split_axis=3, concat_axis=3, tiled=True)
    owned = arrived.reshape(4, per_energy, per_cell, green.shape[3], width)
    whole = ring_gather(green)
    group = lax.axis_index("energy")
    shifts, lives = slot_tables(shift_table, shift_count, group)
    return ring_convolve(shifts, lives, owned, whole, shift_table.shape[2])


def solution(mesh):
    placed = (
        P(None, "energy", "cell", None, None),
        P(None, "energy", None, "cell", None),
        P(),
        P(),
        P(),
    )
    return jax.shard_map(
        per_device,
        mesh=mesh,
        in_specs=placed,
        out_specs=P(None, "energy", "cell", None, None),
        check_vma=False,
    )
```

```python
import functools

import jax
import jax.numpy as jnp
from jax import lax
from jax.experimental import pallas as pl
from jax.experimental.pallas import tpu as pltpu
from jax.sharding import PartitionSpec as P

SCALE = 0.2
LANES = 128


def slot_tables(shift_table, shift_count, group):
    groups, slot_count = shift_table.shape[1], shift_table.shape[2]
    slot = lax.broadcasted_iota(jnp.int32, (groups, slot_count), 1)
    live = (slot < shift_count[group][:, None]).astype(jnp.float32)
    return shift_table[group].reshape(-1), live.reshape(-1)


def ring_conv_kernel(chips, slot_count, shift_ref, live_ref, w_hbm, g_hbm, o_ref, g_vmem, *scratch):
    halves = 2
    count = 2 * chips
    bufs = [scratch[h * count:(h + 1) * count] for h in range(halves)]
    own_bufs = [b[0] for b in bufs]
    ring_bufs = [(None,) + tuple(b[1:chips]) for b in bufs]
    hand_bufs = [tuple(b[chips:count]) for b in bufs]
    g_sem, local_sem, ring_send, ring_recv, pass_send, pass_recv = scratch[halves * count:]
    comps, per_energy, positions, rows, width = o_ref.shape
    me = lax.axis_index("energy")
    cell = lax.axis_index("cell")
    chip, core = me // 2, me % 2
    step_dir = 1 - 2 * core
    partner = me + step_dir
    ahead = 2 * ((chip + step_dir + chips) % chips) + core
    base = me * per_energy

    def origin(k):
        return 2 * ((chip - step_dir * k + chips) % chips) + core

    def handed_group(k):
        return 2 * ((chip + step_dir * k + chips) % chips) + 1 - core

    def own_half(h):
        return w_hbm.at[pl.ds(2 * h, 2)]

    def remote(src, dst, send, recv, k, h, target):
        return pltpu.make_async_remote_copy(
            src_ref=src, dst_ref=dst, send_sem=send.at[k, h], recv_sem=recv.at[k, h],
            device_id=(target, cell), device_id_type=pl.DeviceIdType.MESH,
        )

    def ring_copy(k, h):
        src = own_half(h) if k == 1 else ring_bufs[h][k - 1]
        return remote(src, ring_bufs[h][k], ring_send, ring_recv, k, h, ahead)

    def pass_copy(k, h):
        src = own_half(h) if k == 0 else ring_bufs[h][k]
        return remote(src, hand_bufs[h][k], pass_send, pass_recv, k, h, partner)

    def arrival(k, h):
        return remote(ring_bufs[h][k], ring_bufs[h][k], ring_send, ring_recv, k, h, ahead)

    def handed(k, h):
        return remote(hand_bufs[h][k], hand_bufs[h][k], pass_send, pass_recv, k, h, partner)

    def compute(source, buf, kind, masked):
        lag = base - source * per_energy

        def run():
            for p in range(positions):
                for chunk in range(width // LANES):
                    lanes = pl.ds(chunk * LANES, LANES)

                    def over_energy(e, carry, p=p, lanes=lanes):
                        real = jnp.zeros((rows, LANES), jnp.float32)
                        imag = jnp.zeros((rows, LANES), jnp.float32)
                        for c in range(slot_count):
                            j = shift_ref[source * slot_count + c]
                            weight = live_ref[source * slot_count + c]
                            u = lag + e - j
                            if masked:
                                weight = jnp.where(u >= 0, weight, 0.0)
                                u = jnp.maximum(u, 0)
                            gr = g_vmem[2 * kind, u, p, :, lanes].astype(jnp.float32)
                            gi = g_vmem[2 * kind + 1, u, p, :, lanes].astype(jnp.float32)
                            wr = buf[0, j, p, :, lanes].astype(jnp.float32) * weight
                            wi = buf[1, j, p, :, lanes].astype(jnp.float32) * weight
                            real = real - (gr * wi + gi * wr)
                            imag = imag + (gr * wr - gi * wi)
                        o_ref[2 * kind, e, p, :, lanes] += real
                        o_ref[2 * kind + 1, e, p, :, lanes] += imag
                        return carry

                    lax.fori_loop(0, per_energy, over_energy, 0)

        if masked:
            run()
        else:
            pl.when(source < me)(run)

    g_copy = pltpu.make_async_copy(g_hbm, g_vmem, g_sem)
    g_copy.start()
    locals_ = [pltpu.make_async_copy(own_half(h), own_bufs[h], local_sem.at[h]) for h in range(halves)]
    for copy in locals_:
        copy.start()
    sends = [ring_copy(1, h) for h in range(halves)] + [pass_copy(0, h) for h in range(halves)]
    for copy in sends:
        copy.start()
    o_ref[...] = jnp.zeros(o_ref.shape, o_ref.dtype)
    g_copy.wait()
    for h in range(halves):
        locals_[h].wait()
        compute(me, own_bufs[h], h, True)
    for k in range(1, chips):
        for h in range(halves):
            arrival(k, h).wait_recv()
            onward = [pass_copy(k, h)]
            if k + 1 < chips:
                onward.append(ring_copy(k + 1, h))
            for copy in onward:
                copy.start()
            sends.extend(onward)
            compute(origin(k), ring_bufs[h][k], h, False)
        for h in range(halves):
            handed(k - 1, h).wait_recv()
            compute(handed_group(k - 1), hand_bufs[h][k - 1], h, False)
    for h in range(halves):
        handed(chips - 1, h).wait_recv()
        compute(handed_group(chips - 1), hand_bufs[h][chips - 1], h, False)
    for copy in sends:
        copy.wait_send()
    o_ref[...] = o_ref[...] * SCALE


def ring_convolve(shifts, lives, owned, whole, slot_count):
    groups = lax.axis_size("energy")
    chips = groups // 2
    half = pltpu.VMEM((owned.shape[0] // 2,) + owned.shape[1:], owned.dtype)
    return pl.pallas_call(
        functools.partial(ring_conv_kernel, chips, slot_count),
        out_shape=jax.ShapeDtypeStruct(owned.shape, jnp.float32),
        in_specs=[
            pl.BlockSpec(memory_space=pltpu.SMEM),
            pl.BlockSpec(memory_space=pltpu.SMEM),
            pl.BlockSpec(memory_space=pl.ANY),
            pl.BlockSpec(memory_space=pl.ANY),
        ],
        out_specs=pl.BlockSpec(memory_space=pltpu.VMEM),
        scratch_shapes=[pltpu.VMEM(whole.shape, whole.dtype)]
        + [half] * (4 * chips)
        + [
            pltpu.SemaphoreType.DMA(()),
            pltpu.SemaphoreType.DMA((2,)),
            pltpu.SemaphoreType.DMA((chips, 2)),
            pltpu.SemaphoreType.DMA((chips, 2)),
            pltpu.SemaphoreType.DMA((chips, 2)),
            pltpu.SemaphoreType.DMA((chips, 2)),
        ],
        compiler_params=pltpu.CompilerParams(
            has_side_effects=True, vmem_limit_bytes=48 * 1024 * 1024
        ),
    )(shifts, lives, owned, whole)


def gather_kernel(chips, x_hbm, rows_hbm, out_ref, owned_ref, local_sem, ring_send, ring_recv,
                  pass_send, pass_recv, row_send, row_recv, row_local):
    halves = 2
    per_energy = x_hbm.shape[1]
    me = lax.axis_index("energy")
    cell = lax.axis_index("cell")
    chip, core = me // 2, me % 2
    step_dir = 1 - 2 * core
    partner = me + step_dir
    ahead = 2 * ((chip + step_dir + chips) % chips) + core

    def origin(k):
        return 2 * ((chip - step_dir * k + chips) % chips) + core

    def handed_group(k):
        return 2 * ((chip + step_dir * k + chips) % chips) + 1 - core

    def place(group, h):
        return out_ref.at[pl.ds(2 * h, 2), pl.ds(group * per_energy, per_energy)]

    def own_half(h):
        return x_hbm.at[pl.ds(2 * h, 2)]

    def remote(src, dst, send, recv, k, h, target):
        return pltpu.make_async_remote_copy(
            src_ref=src, dst_ref=dst, send_sem=send.at[k, h], recv_sem=recv.at[k, h],
            device_id=(target, cell), device_id_type=pl.DeviceIdType.MESH,
        )

    def ring_copy(k, h):
        src = own_half(h) if k == 1 else place(origin(k - 1), h)
        return remote(src, place(origin(k - 1), h), ring_send, ring_recv, k, h, ahead)

    def pass_copy(k, h):
        src = own_half(h) if k == 0 else place(origin(k), h)
        return remote(src, place(origin(k), h), pass_send, pass_recv, k, h, partner)

    def arrival(k, h):
        return remote(place(origin(k), h), place(origin(k), h), ring_send, ring_recv, k, h, ahead)

    def handed(k, h):
        slot = place(handed_group(k), h)
        return remote(slot, slot, pass_send, pass_recv, k, h, partner)

    peers = rows_hbm.shape[3]

    def row_copy(d):
        return pltpu.make_async_remote_copy(
            src_ref=rows_hbm.at[:, :, :, pl.ds(d, 1)],
            dst_ref=owned_ref.at[:, :, :, pl.ds(cell, 1)],
            send_sem=row_send.at[d], recv_sem=row_recv.at[cell],
            device_id=(me, d), device_id_type=pl.DeviceIdType.MESH,
        )

    def row_arrival(r):
        return pltpu.make_async_remote_copy(
            src_ref=owned_ref.at[:, :, :, pl.ds(r, 1)],
            dst_ref=owned_ref.at[:, :, :, pl.ds(r, 1)],
            send_sem=row_send.at[r], recv_sem=row_recv.at[r],
            device_id=(me, r), device_id_type=pl.DeviceIdType.MESH,
        )

    own_rows = pltpu.make_async_copy(
        rows_hbm.at[:, :, :, pl.ds(cell, 1)], owned_ref.at[:, :, :, pl.ds(cell, 1)], row_local
    )
    own_rows.start()
    row_sends = []
    for step in range(1, peers):
        copy = row_copy((cell + step) % peers)
        copy.start()
        row_sends.append(copy)

    locals_ = [pltpu.make_async_copy(own_half(h), place(me, h), local_sem.at[h]) for h in range(halves)]
    for copy in locals_:
        copy.start()
    sends = [ring_copy(1, h) for h in range(halves)] + [pass_copy(0, h) for h in range(halves)]
    for copy in sends:
        copy.start()
    for k in range(1, chips):
        for h in range(halves):
            arrival(k, h).wait_recv()
            onward = [pass_copy(k, h)]
            if k + 1 < chips:
                onward.append(ring_copy(k + 1, h))
            for copy in onward:
                copy.start()
            sends.extend(onward)
    for k in range(chips):
        for h in range(halves):
            handed(k, h).wait_recv()
    for step in range(1, peers):
        row_arrival((cell + peers - step) % peers).wait_recv()
    for copy in row_sends:
        copy.wait_send()
    own_rows.wait()
    for copy in sends:
        copy.wait_send()
    for copy in locals_:
        copy.wait()


def ring_gather(block, rows):
    groups = lax.axis_size("energy")
    peers = lax.axis_size("cell")
    chips = groups // 2
    shape = (block.shape[0], groups * block.shape[1]) + block.shape[2:]
    return pl.pallas_call(
        functools.partial(gather_kernel, chips),
        out_shape=(
            jax.ShapeDtypeStruct(shape, block.dtype),
            jax.ShapeDtypeStruct(rows.shape, rows.dtype),
        ),
        in_specs=[pl.BlockSpec(memory_space=pl.ANY)] * 2,
        out_specs=(pl.BlockSpec(memory_space=pl.ANY),) * 2,
        scratch_shapes=[
            pltpu.SemaphoreType.DMA((2,)),
            pltpu.SemaphoreType.DMA((chips, 2)),
            pltpu.SemaphoreType.DMA((chips, 2)),
            pltpu.SemaphoreType.DMA((chips, 2)),
            pltpu.SemaphoreType.DMA((chips, 2)),
            pltpu.SemaphoreType.DMA((peers,)),
            pltpu.SemaphoreType.DMA((peers,)),
            pltpu.SemaphoreType.DMA(()),
        ],
        compiler_params=pltpu.CompilerParams(has_side_effects=True),
    )(block, rows)


def per_device(green, screened, cell_map, shift_table, shift_count):
    cell_count = lax.axis_size("cell")
    per_energy = green.shape[1]
    per_cell = green.shape[2]
    width = green.shape[4]
    wanted = jnp.transpose(cell_map.reshape(cell_count, per_cell)).reshape(-1)
    outgoing = jnp.take(screened, wanted, axis=2)
    outgoing = outgoing.reshape(4, per_energy, per_cell, cell_count, screened.shape[3], width)
    whole, arrived = ring_gather(green, outgoing)
    owned = arrived.reshape(4, per_energy, per_cell, green.shape[3], width)
    group = lax.axis_index("energy")
    shifts, lives = slot_tables(shift_table, shift_count, group)
    return ring_convolve(shifts, lives, owned, whole, shift_table.shape[2])


def solution(mesh):
    placed = (
        P(None, "energy", "cell", None, None),
        P(None, "energy", None, "cell", None),
        P(),
        P(),
        P(),
    )
    return jax.shard_map(
        per_device,
        mesh=mesh,
        in_specs=placed,
        out_specs=P(None, "energy", "cell", None, None),
        check_vma=False,
    )
```

```python
import functools

import jax
import jax.numpy as jnp
from jax import lax
from jax.experimental import pallas as pl
from jax.experimental.pallas import tpu as pltpu
from jax.sharding import PartitionSpec as P

SCALE = 0.2
LANES = 128


def slot_tables(shift_table, shift_count, group):
    groups, slot_count = shift_table.shape[1], shift_table.shape[2]
    slot = lax.broadcasted_iota(jnp.int32, (groups, slot_count), 1)
    live = (slot < shift_count[group][:, None]).astype(jnp.float32)
    return shift_table[group].reshape(-1), live.reshape(-1)


def ring_conv_kernel(chips, slot_count, shift_ref, live_ref, w_hbm, g_hbm, o_ref, g_vmem, *scratch):
    halves = 2
    count = 2 * chips
    bufs = [scratch[h * count:(h + 1) * count] for h in range(halves)]
    own_bufs = [b[0] for b in bufs]
    ring_bufs = [(None,) + tuple(b[1:chips]) for b in bufs]
    hand_bufs = [tuple(b[chips:count]) for b in bufs]
    g_sem, local_sem, ring_send, ring_recv, pass_send, pass_recv = scratch[halves * count:]
    comps, per_energy, positions, rows, width = o_ref.shape
    me = lax.axis_index("energy")
    cell = lax.axis_index("cell")
    chip, core = me // 2, me % 2
    step_dir = 1 - 2 * core
    partner = me + step_dir
    ahead = 2 * ((chip + step_dir + chips) % chips) + core
    base = me * per_energy

    def origin(k):
        return 2 * ((chip - step_dir * k + chips) % chips) + core

    def handed_group(k):
        return 2 * ((chip + step_dir * k + chips) % chips) + 1 - core

    def own_half(h):
        return w_hbm.at[pl.ds(2 * h, 2)]

    def remote(src, dst, send, recv, k, h, target):
        return pltpu.make_async_remote_copy(
            src_ref=src, dst_ref=dst, send_sem=send.at[k, h], recv_sem=recv.at[k, h],
            device_id=(target, cell), device_id_type=pl.DeviceIdType.MESH,
        )

    def ring_copy(k, h):
        src = own_half(h) if k == 1 else ring_bufs[h][k - 1]
        return remote(src, ring_bufs[h][k], ring_send, ring_recv, k, h, ahead)

    def pass_copy(k, h):
        src = own_half(h) if k == 0 else ring_bufs[h][k]
        return remote(src, hand_bufs[h][k], pass_send, pass_recv, k, h, partner)

    def arrival(k, h):
        return remote(ring_bufs[h][k], ring_bufs[h][k], ring_send, ring_recv, k, h, ahead)

    def handed(k, h):
        return remote(hand_bufs[h][k], hand_bufs[h][k], pass_send, pass_recv, k, h, partner)

    def compute(source, buf, kind, masked):
        lag = base - source * per_energy

        def run():
            for p in range(positions):
                for chunk in range(width // LANES):
                    lanes = pl.ds(chunk * LANES, LANES)

                    def over_energy(e, carry, p=p, lanes=lanes):
                        real = jnp.zeros((rows, LANES), jnp.float32)
                        imag = jnp.zeros((rows, LANES), jnp.float32)
                        for c in range(slot_count):
                            j = shift_ref[source * slot_count + c]
                            weight = live_ref[source * slot_count + c]
                            u = lag + e - j
                            if masked:
                                weight = jnp.where(u >= 0, weight, 0.0)
                                u = jnp.maximum(u, 0)
                            gr = g_vmem[2 * kind, u, p, :, lanes].astype(jnp.float32)
                            gi = g_vmem[2 * kind + 1, u, p, :, lanes].astype(jnp.float32)
                            wr = buf[0, j, p, :, lanes].astype(jnp.float32) * weight
                            wi = buf[1, j, p, :, lanes].astype(jnp.float32) * weight
                            real = real - (gr * wi + gi * wr)
                            imag = imag + (gr * wr - gi * wi)
                        o_ref[2 * kind, e, p, :, lanes] += real
                        o_ref[2 * kind + 1, e, p, :, lanes] += imag
                        return carry

                    lax.fori_loop(0, per_energy, over_energy, 0)

        if masked:
            run()
        else:
            pl.when(source < me)(run)

    g_copy = pltpu.make_async_copy(g_hbm, g_vmem, g_sem)
    g_copy.start()
    locals_ = [pltpu.make_async_copy(own_half(h), own_bufs[h], local_sem.at[h]) for h in range(halves)]
    for copy in locals_:
        copy.start()
    sends = [ring_copy(1, h) for h in range(halves)] + [pass_copy(0, h) for h in range(halves)]
    for copy in sends:
        copy.start()
    o_ref[...] = jnp.zeros(o_ref.shape, o_ref.dtype)
    g_copy.wait()
    for h in range(halves):
        locals_[h].wait()
        compute(me, own_bufs[h], h, True)
    for k in range(1, chips):
        for h in range(halves):
            arrival(k, h).wait_recv()
            onward = [pass_copy(k, h)]
            if k + 1 < chips:
                onward.append(ring_copy(k + 1, h))
            for copy in onward:
                copy.start()
            sends.extend(onward)
            compute(origin(k), ring_bufs[h][k], h, False)
        for h in range(halves):
            handed(k - 1, h).wait_recv()
            compute(handed_group(k - 1), hand_bufs[h][k - 1], h, False)
    for h in range(halves):
        handed(chips - 1, h).wait_recv()
        compute(handed_group(chips - 1), hand_bufs[h][chips - 1], h, False)
    for copy in sends:
        copy.wait_send()
    o_ref[...] = o_ref[...] * SCALE


def ring_convolve(shifts, lives, owned, whole, slot_count):
    groups = lax.axis_size("energy")
    chips = groups // 2
    half = pltpu.VMEM((owned.shape[0] // 2,) + owned.shape[1:], owned.dtype)
    return pl.pallas_call(
        functools.partial(ring_conv_kernel, chips, slot_count),
        out_shape=jax.ShapeDtypeStruct(owned.shape, jnp.float32),
        in_specs=[
            pl.BlockSpec(memory_space=pltpu.SMEM),
            pl.BlockSpec(memory_space=pltpu.SMEM),
            pl.BlockSpec(memory_space=pl.ANY),
            pl.BlockSpec(memory_space=pl.ANY),
        ],
        out_specs=pl.BlockSpec(memory_space=pltpu.VMEM),
        scratch_shapes=[pltpu.VMEM(whole.shape, whole.dtype)]
        + [half] * (4 * chips)
        + [
            pltpu.SemaphoreType.DMA(()),
            pltpu.SemaphoreType.DMA((2,)),
            pltpu.SemaphoreType.DMA((chips, 2)),
            pltpu.SemaphoreType.DMA((chips, 2)),
            pltpu.SemaphoreType.DMA((chips, 2)),
            pltpu.SemaphoreType.DMA((chips, 2)),
        ],
        compiler_params=pltpu.CompilerParams(
            has_side_effects=True, vmem_limit_bytes=48 * 1024 * 1024
        ),
    )(shifts, lives, owned, whole)


def gather_kernel(chips, x_hbm, rows_hbm, out_ref, owned_ref, local_sem, ring_send, ring_recv,
                  pass_send, pass_recv, row_send, row_recv, row_local):
    halves = 2
    per_energy = x_hbm.shape[1]
    me = lax.axis_index("energy")
    cell = lax.axis_index("cell")
    chip, core = me // 2, me % 2
    step_dir = 1 - 2 * core
    partner = me + step_dir
    ahead = 2 * ((chip + step_dir + chips) % chips) + core

    def origin(k):
        return 2 * ((chip - step_dir * k + chips) % chips) + core

    def handed_group(k):
        return 2 * ((chip + step_dir * k + chips) % chips) + 1 - core

    def place(group, h):
        return out_ref.at[pl.ds(2 * h, 2), pl.ds(group * per_energy, per_energy)]

    def own_half(h):
        return x_hbm.at[pl.ds(2 * h, 2)]

    def remote(src, dst, send, recv, k, h, target):
        return pltpu.make_async_remote_copy(
            src_ref=src, dst_ref=dst, send_sem=send.at[k, h], recv_sem=recv.at[k, h],
            device_id=(target, cell), device_id_type=pl.DeviceIdType.MESH,
        )

    def ring_copy(k, h):
        src = own_half(h) if k == 1 else place(origin(k - 1), h)
        return remote(src, place(origin(k - 1), h), ring_send, ring_recv, k, h, ahead)

    def pass_copy(k, h):
        src = own_half(h) if k == 0 else place(origin(k), h)
        return remote(src, place(origin(k), h), pass_send, pass_recv, k, h, partner)

    def arrival(k, h):
        return remote(place(origin(k), h), place(origin(k), h), ring_send, ring_recv, k, h, ahead)

    def handed(k, h):
        slot = place(handed_group(k), h)
        return remote(slot, slot, pass_send, pass_recv, k, h, partner)

    peers = rows_hbm.shape[3]

    def row_copy(d):
        return pltpu.make_async_remote_copy(
            src_ref=rows_hbm.at[:, :, :, pl.ds(d, 1)],
            dst_ref=owned_ref.at[:, :, :, pl.ds(cell, 1)],
            send_sem=row_send.at[d], recv_sem=row_recv.at[cell],
            device_id=(me, d), device_id_type=pl.DeviceIdType.MESH,
        )

    def row_arrival(r):
        return pltpu.make_async_remote_copy(
            src_ref=owned_ref.at[:, :, :, pl.ds(r, 1)],
            dst_ref=owned_ref.at[:, :, :, pl.ds(r, 1)],
            send_sem=row_send.at[r], recv_sem=row_recv.at[r],
            device_id=(me, r), device_id_type=pl.DeviceIdType.MESH,
        )

    own_rows = pltpu.make_async_copy(
        rows_hbm.at[:, :, :, pl.ds(cell, 1)], owned_ref.at[:, :, :, pl.ds(cell, 1)], row_local
    )
    own_rows.start()
    row_sends = []
    for step in range(1, peers):
        copy = row_copy((cell + step) % peers)
        copy.start()
        row_sends.append(copy)

    locals_ = [pltpu.make_async_copy(own_half(h), place(me, h), local_sem.at[h]) for h in range(halves)]
    for copy in locals_:
        copy.start()
    sends = [ring_copy(1, h) for h in range(halves)] + [pass_copy(0, h) for h in range(halves)]
    for copy in sends:
        copy.start()
    for k in range(1, chips):
        for h in range(halves):
            arrival(k, h).wait_recv()
            onward = [pass_copy(k, h)]
            if k + 1 < chips:
                onward.append(ring_copy(k + 1, h))
            for copy in onward:
                copy.start()
            sends.extend(onward)
    for k in range(chips):
        for h in range(halves):
            handed(k, h).wait_recv()
    for step in range(1, peers):
        row_arrival((cell + peers - step) % peers).wait_recv()
    for copy in row_sends:
        copy.wait_send()
    own_rows.wait()
    for copy in sends:
        copy.wait_send()
    for copy in locals_:
        copy.wait()


def ring_gather(block, rows):
    groups = lax.axis_size("energy")
    peers = lax.axis_size("cell")
    chips = groups // 2
    shape = (block.shape[0], groups * block.shape[1]) + block.shape[2:]
    return pl.pallas_call(
        functools.partial(gather_kernel, chips),
        out_shape=(
            jax.ShapeDtypeStruct(shape, block.dtype),
            jax.ShapeDtypeStruct(rows.shape, rows.dtype),
        ),
        in_specs=[pl.BlockSpec(memory_space=pl.ANY)] * 2,
        out_specs=(pl.BlockSpec(memory_space=pl.ANY),) * 2,
        scratch_shapes=[
            pltpu.SemaphoreType.DMA((2,)),
            pltpu.SemaphoreType.DMA((chips, 2)),
            pltpu.SemaphoreType.DMA((chips, 2)),
            pltpu.SemaphoreType.DMA((chips, 2)),
            pltpu.SemaphoreType.DMA((chips, 2)),
            pltpu.SemaphoreType.DMA((peers,)),
            pltpu.SemaphoreType.DMA((peers,)),
            pltpu.SemaphoreType.DMA(()),
        ],
        compiler_params=pltpu.CompilerParams(has_side_effects=True),
    )(block, rows)


def per_device(green, screened, cell_map, shift_table, shift_count):
    cell_count = lax.axis_size("cell")
    per_energy = green.shape[1]
    per_cell = green.shape[2]
    width = green.shape[4]
    wanted = jnp.transpose(cell_map.reshape(cell_count, per_cell)).reshape(-1)
    outgoing = jnp.take(screened, wanted, axis=2, mode="clip")
    outgoing = outgoing.reshape(4, per_energy, per_cell, cell_count, screened.shape[3], width)
    whole, arrived = ring_gather(green, outgoing)
    owned = arrived.reshape(4, per_energy, per_cell, green.shape[3], width)
    group = lax.axis_index("energy")
    shifts, lives = slot_tables(shift_table, shift_count, group)
    return ring_convolve(shifts, lives, owned, whole, shift_table.shape[2])


def solution(mesh):
    placed = (
        P(None, "energy", "cell", None, None),
        P(None, "energy", None, "cell", None),
        P(),
        P(),
        P(),
    )
    return jax.shard_map(
        per_device,
        mesh=mesh,
        in_specs=placed,
        out_specs=P(None, "energy", "cell", None, None),
        check_vma=False,
    )
```

```python
import functools

import jax
import jax.numpy as jnp
from jax import lax
from jax.experimental import pallas as pl
from jax.experimental.pallas import tpu as pltpu
from jax.sharding import PartitionSpec as P

SCALE = 0.2
LANES = 128


def slot_tables(shift_table, shift_count, group):
    groups, slot_count = shift_table.shape[1], shift_table.shape[2]
    slot = lax.broadcasted_iota(jnp.int32, (groups, slot_count), 1)
    live = (slot < shift_count[group][:, None]).astype(jnp.float32)
    return shift_table[group].reshape(-1), live.reshape(-1)


def ring_conv_kernel(chips, slot_count, shift_ref, live_ref, w_hbm, g_hbm, o_ref, g_vmem, *scratch):
    halves = 2
    count = 2 * chips
    bufs = [scratch[h * count:(h + 1) * count] for h in range(halves)]
    own_bufs = [b[0] for b in bufs]
    ring_bufs = [(None,) + tuple(b[1:chips]) for b in bufs]
    hand_bufs = [tuple(b[chips:count]) for b in bufs]
    g_sem, local_sem, ring_send, ring_recv, pass_send, pass_recv = scratch[halves * count:]
    comps, per_energy, positions, rows, width = o_ref.shape
    me = lax.axis_index("energy")
    cell = lax.axis_index("cell")
    chip, core = me // 2, me % 2
    step_dir = 1 - 2 * core
    partner = me + step_dir
    ahead = 2 * ((chip + step_dir + chips) % chips) + core
    base = me * per_energy

    def origin(k):
        return 2 * ((chip - step_dir * k + chips) % chips) + core

    def handed_group(k):
        return 2 * ((chip + step_dir * k + chips) % chips) + 1 - core

    def own_half(h):
        return w_hbm.at[pl.ds(2 * h, 2)]

    def remote(src, dst, send, recv, k, h, target):
        return pltpu.make_async_remote_copy(
            src_ref=src, dst_ref=dst, send_sem=send.at[k, h], recv_sem=recv.at[k, h],
            device_id=(target, cell), device_id_type=pl.DeviceIdType.MESH,
        )

    def ring_copy(k, h):
        src = own_half(h) if k == 1 else ring_bufs[h][k - 1]
        return remote(src, ring_bufs[h][k], ring_send, ring_recv, k, h, ahead)

    def pass_copy(k, h):
        src = own_half(h) if k == 0 else ring_bufs[h][k]
        return remote(src, hand_bufs[h][k], pass_send, pass_recv, k, h, partner)

    def arrival(k, h):
        return remote(ring_bufs[h][k], ring_bufs[h][k], ring_send, ring_recv, k, h, ahead)

    def handed(k, h):
        return remote(hand_bufs[h][k], hand_bufs[h][k], pass_send, pass_recv, k, h, partner)

    def compute(source, buf, kind, masked):
        lag = base - source * per_energy

        def run():
            for p in range(positions):
                for chunk in range(width // LANES):
                    lanes = pl.ds(chunk * LANES, LANES)

                    def over_energy(e, carry, p=p, lanes=lanes):
                        real = jnp.zeros((rows, LANES), jnp.float32)
                        imag = jnp.zeros((rows, LANES), jnp.float32)
                        for c in range(slot_count):
                            j = shift_ref[source * slot_count + c]
                            weight = live_ref[source * slot_count + c]
                            u = lag + e - j
                            if masked:
                                weight = jnp.where(u >= 0, weight, 0.0)
                                u = jnp.maximum(u, 0)
                            gr = g_vmem[2 * kind, u, p, :, lanes].astype(jnp.float32)
                            gi = g_vmem[2 * kind + 1, u, p, :, lanes].astype(jnp.float32)
                            wr = buf[0, j, p, :, lanes].astype(jnp.float32) * weight
                            wi = buf[1, j, p, :, lanes].astype(jnp.float32) * weight
                            real = real - (gr * wi + gi * wr)
                            imag = imag + (gr * wr - gi * wi)
                        o_ref[2 * kind, e, p, :, lanes] += real
                        o_ref[2 * kind + 1, e, p, :, lanes] += imag
                        return carry

                    lax.fori_loop(0, per_energy, over_energy, 0)

        if masked:
            run()
        else:
            pl.when(source < me)(run)

    g_copy = pltpu.make_async_copy(g_hbm, g_vmem, g_sem)
    g_copy.start()
    locals_ = [pltpu.make_async_copy(own_half(h), own_bufs[h], local_sem.at[h]) for h in range(halves)]
    for copy in locals_:
        copy.start()
    sends = [ring_copy(1, h) for h in range(halves)] + [pass_copy(0, h) for h in range(halves)]
    for copy in sends:
        copy.start()
    o_ref[...] = jnp.zeros(o_ref.shape, o_ref.dtype)
    g_copy.wait()
    for h in range(halves):
        locals_[h].wait()
        compute(me, own_bufs[h], h, True)
    for k in range(1, chips):
        for h in range(halves):
            arrival(k, h).wait_recv()
            onward = [pass_copy(k, h)]
            if k + 1 < chips:
                onward.append(ring_copy(k + 1, h))
            for copy in onward:
                copy.start()
            sends.extend(onward)
            compute(origin(k), ring_bufs[h][k], h, False)
        for h in range(halves):
            handed(k - 1, h).wait_recv()
            compute(handed_group(k - 1), hand_bufs[h][k - 1], h, False)
    for h in range(halves):
        handed(chips - 1, h).wait_recv()
        compute(handed_group(chips - 1), hand_bufs[h][chips - 1], h, False)
    for copy in sends:
        copy.wait_send()
    o_ref[...] = o_ref[...] * SCALE


def ring_convolve(shifts, lives, owned, whole, slot_count):
    groups = lax.axis_size("energy")
    chips = groups // 2
    half = pltpu.VMEM((owned.shape[0] // 2,) + owned.shape[1:], owned.dtype)
    return pl.pallas_call(
        functools.partial(ring_conv_kernel, chips, slot_count),
        out_shape=jax.ShapeDtypeStruct(owned.shape, jnp.float32),
        in_specs=[
            pl.BlockSpec(memory_space=pltpu.SMEM),
            pl.BlockSpec(memory_space=pltpu.SMEM),
            pl.BlockSpec(memory_space=pl.ANY),
            pl.BlockSpec(memory_space=pl.ANY),
        ],
        out_specs=pl.BlockSpec(memory_space=pltpu.VMEM),
        scratch_shapes=[pltpu.VMEM(whole.shape, whole.dtype)]
        + [half] * (4 * chips)
        + [
            pltpu.SemaphoreType.DMA(()),
            pltpu.SemaphoreType.DMA((2,)),
            pltpu.SemaphoreType.DMA((chips, 2)),
            pltpu.SemaphoreType.DMA((chips, 2)),
            pltpu.SemaphoreType.DMA((chips, 2)),
            pltpu.SemaphoreType.DMA((chips, 2)),
        ],
        compiler_params=pltpu.CompilerParams(
            has_side_effects=True, vmem_limit_bytes=48 * 1024 * 1024
        ),
    )(shifts, lives, owned, whole)


def gather_kernel(chips, x_hbm, rows_hbm, out_ref, owned_ref, local_sem, ring_send, ring_recv,
                  pass_send, pass_recv, row_send, row_recv, row_local):
    halves = 2
    per_energy = x_hbm.shape[1]
    me = lax.axis_index("energy")
    cell = lax.axis_index("cell")
    chip, core = me // 2, me % 2
    step_dir = 1 - 2 * core
    partner = me + step_dir
    ahead = 2 * ((chip + step_dir + chips) % chips) + core

    def origin(k):
        return 2 * ((chip - step_dir * k + chips) % chips) + core

    def handed_group(k):
        return 2 * ((chip + step_dir * k + chips) % chips) + 1 - core

    def place(group, h):
        return out_ref.at[pl.ds(2 * h, 2), pl.ds(group * per_energy, per_energy)]

    def own_half(h):
        return x_hbm.at[pl.ds(2 * h, 2)]

    def remote(src, dst, send, recv, k, h, target):
        return pltpu.make_async_remote_copy(
            src_ref=src, dst_ref=dst, send_sem=send.at[k, h], recv_sem=recv.at[k, h],
            device_id=(target, cell), device_id_type=pl.DeviceIdType.MESH,
        )

    def ring_copy(k, h):
        src = own_half(h) if k == 1 else place(origin(k - 1), h)
        return remote(src, place(origin(k - 1), h), ring_send, ring_recv, k, h, ahead)

    def pass_copy(k, h):
        src = own_half(h) if k == 0 else place(origin(k), h)
        return remote(src, place(origin(k), h), pass_send, pass_recv, k, h, partner)

    def arrival(k, h):
        return remote(place(origin(k), h), place(origin(k), h), ring_send, ring_recv, k, h, ahead)

    def handed(k, h):
        slot = place(handed_group(k), h)
        return remote(slot, slot, pass_send, pass_recv, k, h, partner)

    peers = rows_hbm.shape[0]

    def row_copy(d):
        return pltpu.make_async_remote_copy(
            src_ref=rows_hbm.at[d],
            dst_ref=owned_ref.at[cell],
            send_sem=row_send.at[d], recv_sem=row_recv.at[cell],
            device_id=(me, d), device_id_type=pl.DeviceIdType.MESH,
        )

    def row_arrival(r):
        return pltpu.make_async_remote_copy(
            src_ref=owned_ref.at[r],
            dst_ref=owned_ref.at[r],
            send_sem=row_send.at[r], recv_sem=row_recv.at[r],
            device_id=(me, r), device_id_type=pl.DeviceIdType.MESH,
        )

    own_rows = pltpu.make_async_copy(
        rows_hbm.at[cell], owned_ref.at[cell], row_local
    )
    own_rows.start()
    row_sends = []
    for step in range(1, peers):
        copy = row_copy((cell + step) % peers)
        copy.start()
        row_sends.append(copy)

    locals_ = [pltpu.make_async_copy(own_half(h), place(me, h), local_sem.at[h]) for h in range(halves)]
    for copy in locals_:
        copy.start()
    sends = [ring_copy(1, h) for h in range(halves)] + [pass_copy(0, h) for h in range(halves)]
    for copy in sends:
        copy.start()
    for k in range(1, chips):
        for h in range(halves):
            arrival(k, h).wait_recv()
            onward = [pass_copy(k, h)]
            if k + 1 < chips:
                onward.append(ring_copy(k + 1, h))
            for copy in onward:
                copy.start()
            sends.extend(onward)
    for k in range(chips):
        for h in range(halves):
            handed(k, h).wait_recv()
    for step in range(1, peers):
        row_arrival((cell + peers - step) % peers).wait_recv()
    for copy in row_sends:
        copy.wait_send()
    own_rows.wait()
    for copy in sends:
        copy.wait_send()
    for copy in locals_:
        copy.wait()


def ring_gather(block, rows):
    groups = lax.axis_size("energy")
    peers = lax.axis_size("cell")
    chips = groups // 2
    shape = (block.shape[0], groups * block.shape[1]) + block.shape[2:]
    return pl.pallas_call(
        functools.partial(gather_kernel, chips),
        out_shape=(
            jax.ShapeDtypeStruct(shape, block.dtype),
            jax.ShapeDtypeStruct(rows.shape, rows.dtype),
        ),
        in_specs=[pl.BlockSpec(memory_space=pl.ANY)] * 2,
        out_specs=(pl.BlockSpec(memory_space=pl.ANY),) * 2,
        scratch_shapes=[
            pltpu.SemaphoreType.DMA((2,)),
            pltpu.SemaphoreType.DMA((chips, 2)),
            pltpu.SemaphoreType.DMA((chips, 2)),
            pltpu.SemaphoreType.DMA((chips, 2)),
            pltpu.SemaphoreType.DMA((chips, 2)),
            pltpu.SemaphoreType.DMA((peers,)),
            pltpu.SemaphoreType.DMA((peers,)),
            pltpu.SemaphoreType.DMA(()),
        ],
        compiler_params=pltpu.CompilerParams(has_side_effects=True),
    )(block, rows)


def per_device(green, screened, cell_map, shift_table, shift_count):
    cell_count = lax.axis_size("cell")
    per_energy = green.shape[1]
    per_cell = green.shape[2]
    width = green.shape[4]
    flat = screened.reshape(4, per_energy, screened.shape[2], width)
    picked = jnp.take(flat, cell_map, axis=2)
    picked = picked.reshape(4, per_energy, cell_count, per_cell, width)
    outgoing = jnp.transpose(picked, (2, 0, 1, 3, 4)).reshape(cell_count, -1, width)
    whole, arrived = ring_gather(green, outgoing)
    arrived = arrived.reshape(cell_count, 4, per_energy, per_cell, width)
    owned = jnp.transpose(arrived, (1, 2, 3, 0, 4))
    group = lax.axis_index("energy")
    shifts, lives = slot_tables(shift_table, shift_count, group)
    return ring_convolve(shifts, lives, owned, whole, shift_table.shape[2])


def solution(mesh):
    placed = (
        P(None, "energy", "cell", None, None),
        P(None, "energy", None, "cell", None),
        P(),
        P(),
        P(),
    )
    return jax.shard_map(
        per_device,
        mesh=mesh,
        in_specs=placed,
        out_specs=P(None, "energy", "cell", None, None),
        check_vma=False,
    )
```

```python
import functools

import jax
import jax.numpy as jnp
from jax import lax
from jax.experimental import pallas as pl
from jax.experimental.pallas import tpu as pltpu
from jax.sharding import PartitionSpec as P

SCALE = 0.2
LANES = 128


def ring_conv_kernel(chips, slot_count, shift_ref, count_ref, w_hbm, g_hbm, o_ref, g_vmem, *scratch):
    halves = 2
    count = 2 * chips
    bufs = [scratch[h * count:(h + 1) * count] for h in range(halves)]
    own_bufs = [b[0] for b in bufs]
    ring_bufs = [(None,) + tuple(b[1:chips]) for b in bufs]
    hand_bufs = [tuple(b[chips:count]) for b in bufs]
    g_sem, local_sem, ring_send, ring_recv, pass_send, pass_recv = scratch[halves * count:]
    comps, per_energy, positions, rows, width = o_ref.shape
    me = lax.axis_index("energy")
    cell = lax.axis_index("cell")
    chip, core = me // 2, me % 2
    step_dir = 1 - 2 * core
    partner = me + step_dir
    ahead = 2 * ((chip + step_dir + chips) % chips) + core
    base = me * per_energy
    groups = 2 * chips

    def origin(k):
        return 2 * ((chip - step_dir * k + chips) % chips) + core

    def handed_group(k):
        return 2 * ((chip + step_dir * k + chips) % chips) + 1 - core

    def own_half(h):
        return w_hbm.at[pl.ds(2 * h, 2)]

    def remote(src, dst, send, recv, k, h, target):
        return pltpu.make_async_remote_copy(
            src_ref=src, dst_ref=dst, send_sem=send.at[k, h], recv_sem=recv.at[k, h],
            device_id=(target, cell), device_id_type=pl.DeviceIdType.MESH,
        )

    def ring_copy(k, h):
        src = own_half(h) if k == 1 else ring_bufs[h][k - 1]
        return remote(src, ring_bufs[h][k], ring_send, ring_recv, k, h, ahead)

    def pass_copy(k, h):
        src = own_half(h) if k == 0 else ring_bufs[h][k]
        return remote(src, hand_bufs[h][k], pass_send, pass_recv, k, h, partner)

    def arrival(k, h):
        return remote(ring_bufs[h][k], ring_bufs[h][k], ring_send, ring_recv, k, h, ahead)

    def handed(k, h):
        return remote(hand_bufs[h][k], hand_bufs[h][k], pass_send, pass_recv, k, h, partner)

    def compute(source, buf, kind, masked):
        lag = base - source * per_energy

        def run():
            for p in range(positions):
                for chunk in range(width // LANES):
                    lanes = pl.ds(chunk * LANES, LANES)

                    def over_energy(e, carry, p=p, lanes=lanes):
                        real = jnp.zeros((rows, LANES), jnp.float32)
                        imag = jnp.zeros((rows, LANES), jnp.float32)
                        for c in range(slot_count):
                            j = shift_ref[(me * groups + source) * slot_count + c]
                            live = c < count_ref[me * groups + source]
                            weight = jnp.where(live, 1.0, 0.0).astype(jnp.float32)
                            u = lag + e - j
                            if masked:
                                weight = jnp.where(u >= 0, weight, 0.0)
                                u = jnp.maximum(u, 0)
                            gr = g_vmem[2 * kind, u, p, :, lanes].astype(jnp.float32)
                            gi = g_vmem[2 * kind + 1, u, p, :, lanes].astype(jnp.float32)
                            wr = buf[0, j, p, :, lanes].astype(jnp.float32) * weight
                            wi = buf[1, j, p, :, lanes].astype(jnp.float32) * weight
                            real = real - (gr * wi + gi * wr)
                            imag = imag + (gr * wr - gi * wi)
                        o_ref[2 * kind, e, p, :, lanes] += real
                        o_ref[2 * kind + 1, e, p, :, lanes] += imag
                        return carry

                    lax.fori_loop(0, per_energy, over_energy, 0)

        if masked:
            run()
        else:
            pl.when(source < me)(run)

    g_copy = pltpu.make_async_copy(g_hbm, g_vmem, g_sem)
    g_copy.start()
    locals_ = [pltpu.make_async_copy(own_half(h), own_bufs[h], local_sem.at[h]) for h in range(halves)]
    for copy in locals_:
        copy.start()
    sends = [ring_copy(1, h) for h in range(halves)] + [pass_copy(0, h) for h in range(halves)]
    for copy in sends:
        copy.start()
    o_ref[...] = jnp.zeros(o_ref.shape, o_ref.dtype)
    g_copy.wait()
    for h in range(halves):
        locals_[h].wait()
        compute(me, own_bufs[h], h, True)
    for k in range(1, chips):
        for h in range(halves):
            arrival(k, h).wait_recv()
            onward = [pass_copy(k, h)]
            if k + 1 < chips:
                onward.append(ring_copy(k + 1, h))
            for copy in onward:
                copy.start()
            sends.extend(onward)
            compute(origin(k), ring_bufs[h][k], h, False)
        for h in range(halves):
            handed(k - 1, h).wait_recv()
            compute(handed_group(k - 1), hand_bufs[h][k - 1], h, False)
    for h in range(halves):
        handed(chips - 1, h).wait_recv()
        compute(handed_group(chips - 1), hand_bufs[h][chips - 1], h, False)
    for copy in sends:
        copy.wait_send()
    o_ref[...] = o_ref[...] * SCALE


def ring_convolve(shifts, counts, owned, whole, slot_count):
    groups = lax.axis_size("energy")
    chips = groups // 2
    half = pltpu.VMEM((owned.shape[0] // 2,) + owned.shape[1:], owned.dtype)
    return pl.pallas_call(
        functools.partial(ring_conv_kernel, chips, slot_count),
        out_shape=jax.ShapeDtypeStruct(owned.shape, jnp.float32),
        in_specs=[
            pl.BlockSpec(memory_space=pltpu.SMEM),
            pl.BlockSpec(memory_space=pltpu.SMEM),
            pl.BlockSpec(memory_space=pl.ANY),
            pl.BlockSpec(memory_space=pl.ANY),
        ],
        out_specs=pl.BlockSpec(memory_space=pltpu.VMEM),
        scratch_shapes=[pltpu.VMEM(whole.shape, whole.dtype)]
        + [half] * (4 * chips)
        + [
            pltpu.SemaphoreType.DMA(()),
            pltpu.SemaphoreType.DMA((2,)),
            pltpu.SemaphoreType.DMA((chips, 2)),
            pltpu.SemaphoreType.DMA((chips, 2)),
            pltpu.SemaphoreType.DMA((chips, 2)),
            pltpu.SemaphoreType.DMA((chips, 2)),
        ],
        compiler_params=pltpu.CompilerParams(
            has_side_effects=True, vmem_limit_bytes=48 * 1024 * 1024
        ),
    )(shifts, counts, owned, whole)


def gather_kernel(chips, x_hbm, rows_hbm, out_ref, owned_ref, local_sem, ring_send, ring_recv,
                  pass_send, pass_recv, row_send, row_recv, row_local):
    halves = 2
    per_energy = x_hbm.shape[1]
    me = lax.axis_index("energy")
    cell = lax.axis_index("cell")
    chip, core = me // 2, me % 2
    step_dir = 1 - 2 * core
    partner = me + step_dir
    ahead = 2 * ((chip + step_dir + chips) % chips) + core

    def origin(k):
        return 2 * ((chip - step_dir * k + chips) % chips) + core

    def handed_group(k):
        return 2 * ((chip + step_dir * k + chips) % chips) + 1 - core

    def place(group, h):
        return out_ref.at[pl.ds(2 * h, 2), pl.ds(group * per_energy, per_energy)]

    def own_half(h):
        return x_hbm.at[pl.ds(2 * h, 2)]

    def remote(src, dst, send, recv, k, h, target):
        return pltpu.make_async_remote_copy(
            src_ref=src, dst_ref=dst, send_sem=send.at[k, h], recv_sem=recv.at[k, h],
            device_id=(target, cell), device_id_type=pl.DeviceIdType.MESH,
        )

    def ring_copy(k, h):
        src = own_half(h) if k == 1 else place(origin(k - 1), h)
        return remote(src, place(origin(k - 1), h), ring_send, ring_recv, k, h, ahead)

    def pass_copy(k, h):
        src = own_half(h) if k == 0 else place(origin(k), h)
        return remote(src, place(origin(k), h), pass_send, pass_recv, k, h, partner)

    def arrival(k, h):
        return remote(place(origin(k), h), place(origin(k), h), ring_send, ring_recv, k, h, ahead)

    def handed(k, h):
        slot = place(handed_group(k), h)
        return remote(slot, slot, pass_send, pass_recv, k, h, partner)

    peers = rows_hbm.shape[0]

    def row_copy(d):
        return pltpu.make_async_remote_copy(
            src_ref=rows_hbm.at[d],
            dst_ref=owned_ref.at[cell],
            send_sem=row_send.at[d], recv_sem=row_recv.at[cell],
            device_id=(me, d), device_id_type=pl.DeviceIdType.MESH,
        )

    def row_arrival(r):
        return pltpu.make_async_remote_copy(
            src_ref=owned_ref.at[r],
            dst_ref=owned_ref.at[r],
            send_sem=row_send.at[r], recv_sem=row_recv.at[r],
            device_id=(me, r), device_id_type=pl.DeviceIdType.MESH,
        )

    own_rows = pltpu.make_async_copy(
        rows_hbm.at[cell], owned_ref.at[cell], row_local
    )
    own_rows.start()
    row_sends = []
    for step in range(1, peers):
        copy = row_copy((cell + step) % peers)
        copy.start()
        row_sends.append(copy)

    locals_ = [pltpu.make_async_copy(own_half(h), place(me, h), local_sem.at[h]) for h in range(halves)]
    for copy in locals_:
        copy.start()
    sends = [ring_copy(1, h) for h in range(halves)] + [pass_copy(0, h) for h in range(halves)]
    for copy in sends:
        copy.start()
    for k in range(1, chips):
        for h in range(halves):
            arrival(k, h).wait_recv()
            onward = [pass_copy(k, h)]
            if k + 1 < chips:
                onward.append(ring_copy(k + 1, h))
            for copy in onward:
                copy.start()
            sends.extend(onward)
    for k in range(chips):
        for h in range(halves):
            handed(k, h).wait_recv()
    for step in range(1, peers):
        row_arrival((cell + peers - step) % peers).wait_recv()
    for copy in row_sends:
        copy.wait_send()
    own_rows.wait()
    for copy in sends:
        copy.wait_send()
    for copy in locals_:
        copy.wait()


def ring_gather(block, rows):
    groups = lax.axis_size("energy")
    peers = lax.axis_size("cell")
    chips = groups // 2
    shape = (block.shape[0], groups * block.shape[1]) + block.shape[2:]
    return pl.pallas_call(
        functools.partial(gather_kernel, chips),
        out_shape=(
            jax.ShapeDtypeStruct(shape, block.dtype),
            jax.ShapeDtypeStruct(rows.shape, rows.dtype),
        ),
        in_specs=[pl.BlockSpec(memory_space=pl.ANY)] * 2,
        out_specs=(pl.BlockSpec(memory_space=pl.ANY),) * 2,
        scratch_shapes=[
            pltpu.SemaphoreType.DMA((2,)),
            pltpu.SemaphoreType.DMA((chips, 2)),
            pltpu.SemaphoreType.DMA((chips, 2)),
            pltpu.SemaphoreType.DMA((chips, 2)),
            pltpu.SemaphoreType.DMA((chips, 2)),
            pltpu.SemaphoreType.DMA((peers,)),
            pltpu.SemaphoreType.DMA((peers,)),
            pltpu.SemaphoreType.DMA(()),
        ],
        compiler_params=pltpu.CompilerParams(has_side_effects=True),
    )(block, rows)


def per_device(green, screened, cell_map, shift_table, shift_count):
    cell_count = lax.axis_size("cell")
    per_energy = green.shape[1]
    per_cell = green.shape[2]
    width = green.shape[4]
    flat = screened.reshape(4, per_energy, screened.shape[2], width)
    picked = jnp.take(flat, cell_map, axis=2, mode="clip")
    picked = picked.reshape(4, per_energy, cell_count, per_cell, width)
    outgoing = jnp.transpose(picked, (2, 0, 1, 3, 4)).reshape(cell_count, -1, width)
    whole, arrived = ring_gather(green, outgoing)
    arrived = arrived.reshape(cell_count, 4, per_energy, per_cell, width)
    owned = jnp.transpose(arrived, (1, 2, 3, 0, 4))
    return ring_convolve(
        shift_table.reshape(-1), shift_count.reshape(-1), owned, whole, shift_table.shape[2]
    )


def solution(mesh):
    placed = (
        P(None, "energy", "cell", None, None),
        P(None, "energy", None, "cell", None),
        P(),
        P(),
        P(),
    )
    return jax.shard_map(
        per_device,
        mesh=mesh,
        in_specs=placed,
        out_specs=P(None, "energy", "cell", None, None),
        check_vma=False,
    )
```

```python
import functools

import jax
import jax.numpy as jnp
from jax import lax
from jax.experimental import pallas as pl
from jax.experimental.pallas import tpu as pltpu
from jax.sharding import PartitionSpec as P

SCALE = 0.2
LANES = 128


def slot_tables(shift_table, shift_count, group):
    groups, slot_count = shift_table.shape[1], shift_table.shape[2]
    slot = lax.broadcasted_iota(jnp.int32, (groups, slot_count), 1)
    live = (slot < shift_count[group][:, None]).astype(jnp.float32)
    return shift_table[group].reshape(-1), live.reshape(-1)


def ring_conv_kernel(chips, slot_count, shift_ref, live_ref, w_hbm, g_hbm, out_hbm, o_ref, g_vmem, *scratch):
    halves = 2
    count = 2 * chips
    bufs = [scratch[h * count:(h + 1) * count] for h in range(halves)]
    own_bufs = [b[0] for b in bufs]
    ring_bufs = [(None,) + tuple(b[1:chips]) for b in bufs]
    hand_bufs = [tuple(b[chips:count]) for b in bufs]
    g_sem, local_sem, ring_send, ring_recv, pass_send, pass_recv, out_sem = scratch[halves * count:]
    comps, per_energy, positions, rows, width = o_ref.shape
    me = lax.axis_index("energy")
    cell = lax.axis_index("cell")
    chip, core = me // 2, me % 2
    step_dir = 1 - 2 * core
    partner = me + step_dir
    ahead = 2 * ((chip + step_dir + chips) % chips) + core
    base = me * per_energy

    def origin(k):
        return 2 * ((chip - step_dir * k + chips) % chips) + core

    def handed_group(k):
        return 2 * ((chip + step_dir * k + chips) % chips) + 1 - core

    def own_half(h):
        return w_hbm.at[pl.ds(2 * h, 2)]

    def remote(src, dst, send, recv, k, h, target):
        return pltpu.make_async_remote_copy(
            src_ref=src, dst_ref=dst, send_sem=send.at[k, h], recv_sem=recv.at[k, h],
            device_id=(target, cell), device_id_type=pl.DeviceIdType.MESH,
        )

    def ring_copy(k, h):
        src = own_half(h) if k == 1 else ring_bufs[h][k - 1]
        return remote(src, ring_bufs[h][k], ring_send, ring_recv, k, h, ahead)

    def pass_copy(k, h):
        src = own_half(h) if k == 0 else ring_bufs[h][k]
        return remote(src, hand_bufs[h][k], pass_send, pass_recv, k, h, partner)

    def arrival(k, h):
        return remote(ring_bufs[h][k], ring_bufs[h][k], ring_send, ring_recv, k, h, ahead)

    def handed(k, h):
        return remote(hand_bufs[h][k], hand_bufs[h][k], pass_send, pass_recv, k, h, partner)

    def compute(source, buf, kind, masked):
        lag = base - source * per_energy

        def run():
            for p in range(positions):
                for chunk in range(width // LANES):
                    lanes = pl.ds(chunk * LANES, LANES)

                    def over_energy(e, carry, p=p, lanes=lanes):
                        real = jnp.zeros((rows, LANES), jnp.float32)
                        imag = jnp.zeros((rows, LANES), jnp.float32)
                        for c in range(slot_count):
                            j = shift_ref[source * slot_count + c]
                            weight = live_ref[source * slot_count + c]
                            u = lag + e - j
                            if masked:
                                weight = jnp.where(u >= 0, weight, 0.0)
                                u = jnp.maximum(u, 0)
                            gr = g_vmem[2 * kind, u, p, :, lanes].astype(jnp.float32)
                            gi = g_vmem[2 * kind + 1, u, p, :, lanes].astype(jnp.float32)
                            wr = buf[0, j, p, :, lanes].astype(jnp.float32) * weight
                            wi = buf[1, j, p, :, lanes].astype(jnp.float32) * weight
                            real = real - (gr * wi + gi * wr)
                            imag = imag + (gr * wr - gi * wi)
                        o_ref[2 * kind, e, p, :, lanes] += real
                        o_ref[2 * kind + 1, e, p, :, lanes] += imag
                        return carry

                    lax.fori_loop(0, per_energy, over_energy, 0)

        if masked:
            run()
        else:
            pl.when(source < me)(run)

    g_copy = pltpu.make_async_copy(g_hbm, g_vmem, g_sem)
    g_copy.start()
    locals_ = [pltpu.make_async_copy(own_half(h), own_bufs[h], local_sem.at[h]) for h in range(halves)]
    for copy in locals_:
        copy.start()
    sends = [ring_copy(1, h) for h in range(halves)] + [pass_copy(0, h) for h in range(halves)]
    for copy in sends:
        copy.start()
    o_ref[...] = jnp.zeros(o_ref.shape, o_ref.dtype)
    g_copy.wait()
    for h in range(halves):
        locals_[h].wait()
        compute(me, own_bufs[h], h, True)
    for k in range(1, chips):
        for h in range(halves):
            arrival(k, h).wait_recv()
            onward = [pass_copy(k, h)]
            if k + 1 < chips:
                onward.append(ring_copy(k + 1, h))
            for copy in onward:
                copy.start()
            sends.extend(onward)
            compute(origin(k), ring_bufs[h][k], h, False)
        for h in range(halves):
            handed(k - 1, h).wait_recv()
            compute(handed_group(k - 1), hand_bufs[h][k - 1], h, False)
    outs = []
    for h in range(halves):
        handed(chips - 1, h).wait_recv()
        compute(handed_group(chips - 1), hand_bufs[h][chips - 1], h, False)
        kind = pl.ds(2 * h, 2)
        o_ref[kind] = o_ref[kind] * SCALE
        copy = pltpu.make_async_copy(o_ref.at[kind], out_hbm.at[kind], out_sem.at[h])
        copy.start()
        outs.append(copy)
    for copy in sends:
        copy.wait_send()
    for copy in outs:
        copy.wait()


def ring_convolve(shifts, lives, owned, whole, slot_count):
    groups = lax.axis_size("energy")
    chips = groups // 2
    half = pltpu.VMEM((owned.shape[0] // 2,) + owned.shape[1:], owned.dtype)
    return pl.pallas_call(
        functools.partial(ring_conv_kernel, chips, slot_count),
        out_shape=jax.ShapeDtypeStruct(owned.shape, jnp.float32),
        in_specs=[
            pl.BlockSpec(memory_space=pltpu.SMEM),
            pl.BlockSpec(memory_space=pltpu.SMEM),
            pl.BlockSpec(memory_space=pl.ANY),
            pl.BlockSpec(memory_space=pl.ANY),
        ],
        out_specs=pl.BlockSpec(memory_space=pl.ANY),
        scratch_shapes=[pltpu.VMEM(owned.shape, jnp.float32), pltpu.VMEM(whole.shape, whole.dtype)]
        + [half] * (4 * chips)
        + [
            pltpu.SemaphoreType.DMA(()),
            pltpu.SemaphoreType.DMA((2,)),
            pltpu.SemaphoreType.DMA((chips, 2)),
            pltpu.SemaphoreType.DMA((chips, 2)),
            pltpu.SemaphoreType.DMA((chips, 2)),
            pltpu.SemaphoreType.DMA((chips, 2)),
            pltpu.SemaphoreType.DMA((2,)),
        ],
        compiler_params=pltpu.CompilerParams(
            has_side_effects=True, vmem_limit_bytes=48 * 1024 * 1024
        ),
    )(shifts, lives, owned, whole)


def gather_kernel(chips, x_hbm, rows_hbm, out_ref, owned_ref, local_sem, ring_send, ring_recv,
                  pass_send, pass_recv, row_send, row_recv, row_local):
    halves = 2
    per_energy = x_hbm.shape[1]
    me = lax.axis_index("energy")
    cell = lax.axis_index("cell")
    chip, core = me // 2, me % 2
    step_dir = 1 - 2 * core
    partner = me + step_dir
    ahead = 2 * ((chip + step_dir + chips) % chips) + core

    def origin(k):
        return 2 * ((chip - step_dir * k + chips) % chips) + core

    def handed_group(k):
        return 2 * ((chip + step_dir * k + chips) % chips) + 1 - core

    def place(group, h):
        return out_ref.at[pl.ds(2 * h, 2), pl.ds(group * per_energy, per_energy)]

    def own_half(h):
        return x_hbm.at[pl.ds(2 * h, 2)]

    def remote(src, dst, send, recv, k, h, target):
        return pltpu.make_async_remote_copy(
            src_ref=src, dst_ref=dst, send_sem=send.at[k, h], recv_sem=recv.at[k, h],
            device_id=(target, cell), device_id_type=pl.DeviceIdType.MESH,
        )

    def ring_copy(k, h):
        src = own_half(h) if k == 1 else place(origin(k - 1), h)
        return remote(src, place(origin(k - 1), h), ring_send, ring_recv, k, h, ahead)

    def pass_copy(k, h):
        src = own_half(h) if k == 0 else place(origin(k), h)
        return remote(src, place(origin(k), h), pass_send, pass_recv, k, h, partner)

    def arrival(k, h):
        return remote(place(origin(k), h), place(origin(k), h), ring_send, ring_recv, k, h, ahead)

    def handed(k, h):
        slot = place(handed_group(k), h)
        return remote(slot, slot, pass_send, pass_recv, k, h, partner)

    peers = rows_hbm.shape[0]

    def row_copy(d):
        return pltpu.make_async_remote_copy(
            src_ref=rows_hbm.at[d],
            dst_ref=owned_ref.at[cell],
            send_sem=row_send.at[d], recv_sem=row_recv.at[cell],
            device_id=(me, d), device_id_type=pl.DeviceIdType.MESH,
        )

    def row_arrival(r):
        return pltpu.make_async_remote_copy(
            src_ref=owned_ref.at[r],
            dst_ref=owned_ref.at[r],
            send_sem=row_send.at[r], recv_sem=row_recv.at[r],
            device_id=(me, r), device_id_type=pl.DeviceIdType.MESH,
        )

    own_rows = pltpu.make_async_copy(
        rows_hbm.at[cell], owned_ref.at[cell], row_local
    )
    own_rows.start()
    row_sends = []
    for step in range(1, peers):
        copy = row_copy((cell + step) % peers)
        copy.start()
        row_sends.append(copy)

    locals_ = [pltpu.make_async_copy(own_half(h), place(me, h), local_sem.at[h]) for h in range(halves)]
    for copy in locals_:
        copy.start()
    sends = [ring_copy(1, h) for h in range(halves)] + [pass_copy(0, h) for h in range(halves)]
    for copy in sends:
        copy.start()
    for k in range(1, chips):
        for h in range(halves):
            arrival(k, h).wait_recv()
            onward = [pass_copy(k, h)]
            if k + 1 < chips:
                onward.append(ring_copy(k + 1, h))
            for copy in onward:
                copy.start()
            sends.extend(onward)
    for k in range(chips):
        for h in range(halves):
            handed(k, h).wait_recv()
    for step in range(1, peers):
        row_arrival((cell + peers - step) % peers).wait_recv()
    for copy in row_sends:
        copy.wait_send()
    own_rows.wait()
    for copy in sends:
        copy.wait_send()
    for copy in locals_:
        copy.wait()


def ring_gather(block, rows):
    groups = lax.axis_size("energy")
    peers = lax.axis_size("cell")
    chips = groups // 2
    shape = (block.shape[0], groups * block.shape[1]) + block.shape[2:]
    return pl.pallas_call(
        functools.partial(gather_kernel, chips),
        out_shape=(
            jax.ShapeDtypeStruct(shape, block.dtype),
            jax.ShapeDtypeStruct(rows.shape, rows.dtype),
        ),
        in_specs=[pl.BlockSpec(memory_space=pl.ANY)] * 2,
        out_specs=(pl.BlockSpec(memory_space=pl.ANY),) * 2,
        scratch_shapes=[
            pltpu.SemaphoreType.DMA((2,)),
            pltpu.SemaphoreType.DMA((chips, 2)),
            pltpu.SemaphoreType.DMA((chips, 2)),
            pltpu.SemaphoreType.DMA((chips, 2)),
            pltpu.SemaphoreType.DMA((chips, 2)),
            pltpu.SemaphoreType.DMA((peers,)),
            pltpu.SemaphoreType.DMA((peers,)),
            pltpu.SemaphoreType.DMA(()),
        ],
        compiler_params=pltpu.CompilerParams(has_side_effects=True),
    )(block, rows)


def per_device(green, screened, cell_map, shift_table, shift_count):
    cell_count = lax.axis_size("cell")
    per_energy = green.shape[1]
    per_cell = green.shape[2]
    width = green.shape[4]
    flat = screened.reshape(4, per_energy, screened.shape[2], width)
    picked = jnp.take(flat, cell_map, axis=2)
    picked = picked.reshape(4, per_energy, cell_count, per_cell, width)
    outgoing = jnp.transpose(picked, (2, 0, 1, 3, 4)).reshape(cell_count, -1, width)
    whole, arrived = ring_gather(green, outgoing)
    arrived = arrived.reshape(cell_count, 4, per_energy, per_cell, width)
    owned = jnp.transpose(arrived, (1, 2, 3, 0, 4))
    group = lax.axis_index("energy")
    shifts, lives = slot_tables(shift_table, shift_count, group)
    return ring_convolve(shifts, lives, owned, whole, shift_table.shape[2])


def solution(mesh):
    placed = (
        P(None, "energy", "cell", None, None),
        P(None, "energy", None, "cell", None),
        P(),
        P(),
        P(),
    )
    return jax.shard_map(
        per_device,
        mesh=mesh,
        in_specs=placed,
        out_specs=P(None, "energy", "cell", None, None),
        check_vma=False,
    )
```

```python
import functools

import jax
import jax.numpy as jnp
from jax import lax
from jax.experimental import pallas as pl
from jax.experimental.pallas import tpu as pltpu
from jax.sharding import PartitionSpec as P

SCALE = 0.2
LANES = 128


def slot_tables(shift_table, shift_count, group):
    groups, slot_count = shift_table.shape[1], shift_table.shape[2]
    slot = lax.broadcasted_iota(jnp.int32, (groups, slot_count), 1)
    live = (slot < shift_count[group][:, None]).astype(jnp.float32)
    return shift_table[group].reshape(-1), live.reshape(-1)


def ring_conv_kernel(chips, slot_count, shift_ref, live_ref, w_hbm, g_hbm, o_ref, g_vmem, *scratch):
    halves = 2
    count = 2 * chips
    bufs = [scratch[h * count:(h + 1) * count] for h in range(halves)]
    own_bufs = [b[0] for b in bufs]
    ring_bufs = [(None,) + tuple(b[1:chips]) for b in bufs]
    hand_bufs = [tuple(b[chips:count]) for b in bufs]
    g_sem, local_sem, ring_send, ring_recv, pass_send, pass_recv = scratch[halves * count:]
    comps, per_energy, positions, rows, width = o_ref.shape
    me = lax.axis_index("energy")
    cell = lax.axis_index("cell")
    chip, core = me // 2, me % 2
    step_dir = 1 - 2 * core
    partner = me + step_dir
    ahead = 2 * ((chip + step_dir + chips) % chips) + core
    base = me * per_energy

    def origin(k):
        return 2 * ((chip - step_dir * k + chips) % chips) + core

    def handed_group(k):
        return 2 * ((chip + step_dir * k + chips) % chips) + 1 - core

    def own_half(h):
        return w_hbm.at[pl.ds(2 * h, 2)]

    def remote(src, dst, send, recv, k, h, target):
        return pltpu.make_async_remote_copy(
            src_ref=src, dst_ref=dst, send_sem=send.at[k, h], recv_sem=recv.at[k, h],
            device_id=(target, cell), device_id_type=pl.DeviceIdType.MESH,
        )

    def ring_copy(k, h):
        src = own_half(h) if k == 1 else ring_bufs[h][k - 1]
        return remote(src, ring_bufs[h][k], ring_send, ring_recv, k, h, ahead)

    def pass_copy(k, h):
        src = own_half(h) if k == 0 else ring_bufs[h][k]
        return remote(src, hand_bufs[h][k], pass_send, pass_recv, k, h, partner)

    def arrival(k, h):
        return remote(ring_bufs[h][k], ring_bufs[h][k], ring_send, ring_recv, k, h, ahead)

    def handed(k, h):
        return remote(hand_bufs[h][k], hand_bufs[h][k], pass_send, pass_recv, k, h, partner)

    def compute(source, buf, kind, masked):
        lag = base - source * per_energy

        def run():
            for p in range(positions):
                for chunk in range(width // LANES):
                    lanes = pl.ds(chunk * LANES, LANES)

                    def over_energy(e, carry, p=p, lanes=lanes):
                        real = jnp.zeros((rows, LANES), jnp.float32)
                        imag = jnp.zeros((rows, LANES), jnp.float32)
                        for c in range(slot_count):
                            j = shift_ref[source * slot_count + c]
                            weight = live_ref[source * slot_count + c]
                            u = lag + e - j
                            if masked:
                                weight = jnp.where(u >= 0, weight, 0.0)
                                u = jnp.maximum(u, 0)
                            gr = g_vmem[2 * kind, u, p, :, lanes].astype(jnp.float32)
                            gi = g_vmem[2 * kind + 1, u, p, :, lanes].astype(jnp.float32)
                            wr = buf[0, j, p, :, lanes].astype(jnp.float32) * weight
                            wi = buf[1, j, p, :, lanes].astype(jnp.float32) * weight
                            real = real - (gr * wi + gi * wr)
                            imag = imag + (gr * wr - gi * wi)
                        o_ref[2 * kind, e, p, :, lanes] += real
                        o_ref[2 * kind + 1, e, p, :, lanes] += imag
                        return carry

                    lax.fori_loop(0, per_energy, over_energy, 0)

        if masked:
            run()
        else:
            pl.when(source < me)(run)

    g_copy = pltpu.make_async_copy(g_hbm, g_vmem, g_sem)
    g_copy.start()
    locals_ = [pltpu.make_async_copy(own_half(h), own_bufs[h], local_sem.at[h]) for h in range(halves)]
    for copy in locals_:
        copy.start()
    sends = [ring_copy(1, h) for h in range(halves)] + [pass_copy(0, h) for h in range(halves)]
    for copy in sends:
        copy.start()
    o_ref[...] = jnp.zeros(o_ref.shape, o_ref.dtype)
    g_copy.wait()
    for h in range(halves):
        locals_[h].wait()
        compute(me, own_bufs[h], h, True)
    for k in range(1, chips):
        for h in range(halves):
            arrival(k, h).wait_recv()
            onward = [pass_copy(k, h)]
            if k + 1 < chips:
                onward.append(ring_copy(k + 1, h))
            for copy in onward:
                copy.start()
            sends.extend(onward)
            compute(origin(k), ring_bufs[h][k], h, False)
        for h in range(halves):
            handed(k - 1, h).wait_recv()
            compute(handed_group(k - 1), hand_bufs[h][k - 1], h, False)
    for h in range(halves):
        handed(chips - 1, h).wait_recv()
        compute(handed_group(chips - 1), hand_bufs[h][chips - 1], h, False)
    for copy in sends:
        copy.wait_send()
    o_ref[...] = o_ref[...] * SCALE


def ring_convolve(shifts, lives, owned, whole, slot_count):
    groups = lax.axis_size("energy")
    chips = groups // 2
    half = pltpu.VMEM((owned.shape[0] // 2,) + owned.shape[1:], owned.dtype)
    return pl.pallas_call(
        functools.partial(ring_conv_kernel, chips, slot_count),
        out_shape=jax.ShapeDtypeStruct(owned.shape, jnp.float32),
        in_specs=[
            pl.BlockSpec(memory_space=pltpu.SMEM),
            pl.BlockSpec(memory_space=pltpu.SMEM),
            pl.BlockSpec(memory_space=pl.ANY),
            pl.BlockSpec(memory_space=pl.ANY),
        ],
        out_specs=pl.BlockSpec(memory_space=pltpu.VMEM),
        scratch_shapes=[pltpu.VMEM(whole.shape, whole.dtype)]
        + [half] * (4 * chips)
        + [
            pltpu.SemaphoreType.DMA(()),
            pltpu.SemaphoreType.DMA((2,)),
            pltpu.SemaphoreType.DMA((chips, 2)),
            pltpu.SemaphoreType.DMA((chips, 2)),
            pltpu.SemaphoreType.DMA((chips, 2)),
            pltpu.SemaphoreType.DMA((chips, 2)),
        ],
        compiler_params=pltpu.CompilerParams(
            has_side_effects=True, vmem_limit_bytes=48 * 1024 * 1024
        ),
    )(shifts, lives, owned, whole)


def gather_kernel(chips, x_hbm, rows_hbm, out_ref, owned_ref, local_sem, ring_send, ring_recv,
                  pass_send, pass_recv, row_send, row_recv, row_local):
    halves = 2
    per_energy = x_hbm.shape[1]
    me = lax.axis_index("energy")
    cell = lax.axis_index("cell")
    chip, core = me // 2, me % 2
    step_dir = 1 - 2 * core
    partner = me + step_dir
    ahead = 2 * ((chip + step_dir + chips) % chips) + core

    def origin(k):
        return 2 * ((chip - step_dir * k + chips) % chips) + core

    def handed_group(k):
        return 2 * ((chip + step_dir * k + chips) % chips) + 1 - core

    def place(group, h):
        return out_ref.at[pl.ds(2 * h, 2), pl.ds(group * per_energy, per_energy)]

    def own_half(h):
        return x_hbm.at[pl.ds(2 * h, 2)]

    def remote(src, dst, send, recv, k, h, target):
        return pltpu.make_async_remote_copy(
            src_ref=src, dst_ref=dst, send_sem=send.at[k, h], recv_sem=recv.at[k, h],
            device_id=(target, cell), device_id_type=pl.DeviceIdType.MESH,
        )

    def ring_copy(k, h):
        src = own_half(h) if k == 1 else place(origin(k - 1), h)
        return remote(src, place(origin(k - 1), h), ring_send, ring_recv, k, h, ahead)

    def pass_copy(k, h):
        src = own_half(h) if k == 0 else place(origin(k), h)
        return remote(src, place(origin(k), h), pass_send, pass_recv, k, h, partner)

    def arrival(k, h):
        return remote(place(origin(k), h), place(origin(k), h), ring_send, ring_recv, k, h, ahead)

    def handed(k, h):
        slot = place(handed_group(k), h)
        return remote(slot, slot, pass_send, pass_recv, k, h, partner)

    peers = rows_hbm.shape[0]

    def row_copy(d):
        return pltpu.make_async_remote_copy(
            src_ref=rows_hbm.at[d],
            dst_ref=owned_ref.at[cell],
            send_sem=row_send.at[d], recv_sem=row_recv.at[cell],
            device_id=(me, d), device_id_type=pl.DeviceIdType.MESH,
        )

    def row_arrival(r):
        return pltpu.make_async_remote_copy(
            src_ref=owned_ref.at[r],
            dst_ref=owned_ref.at[r],
            send_sem=row_send.at[r], recv_sem=row_recv.at[r],
            device_id=(me, r), device_id_type=pl.DeviceIdType.MESH,
        )

    own_rows = pltpu.make_async_copy(
        rows_hbm.at[cell], owned_ref.at[cell], row_local
    )
    own_rows.start()
    row_sends = []
    for step in range(1, peers):
        copy = row_copy((cell + step) % peers)
        copy.start()
        row_sends.append(copy)

    locals_ = [pltpu.make_async_copy(own_half(h), place(me, h), local_sem.at[h]) for h in range(halves)]
    for copy in locals_:
        copy.start()
    sends = [ring_copy(1, h) for h in range(halves)] + [pass_copy(0, h) for h in range(halves)]
    for copy in sends:
        copy.start()
    for k in range(1, chips):
        for h in range(halves):
            arrival(k, h).wait_recv()
            onward = [pass_copy(k, h)]
            if k + 1 < chips:
                onward.append(ring_copy(k + 1, h))
            for copy in onward:
                copy.start()
            sends.extend(onward)
    for k in range(chips):
        for h in range(halves):
            handed(k, h).wait_recv()
    for step in range(1, peers):
        row_arrival((cell + peers - step) % peers).wait_recv()
    for copy in row_sends:
        copy.wait_send()
    own_rows.wait()
    for copy in sends:
        copy.wait_send()
    for copy in locals_:
        copy.wait()


def ring_gather(block, rows):
    groups = lax.axis_size("energy")
    peers = lax.axis_size("cell")
    chips = groups // 2
    shape = (block.shape[0], groups * block.shape[1]) + block.shape[2:]
    return pl.pallas_call(
        functools.partial(gather_kernel, chips),
        out_shape=(
            jax.ShapeDtypeStruct(shape, block.dtype),
            jax.ShapeDtypeStruct(rows.shape, rows.dtype),
        ),
        in_specs=[pl.BlockSpec(memory_space=pl.ANY)] * 2,
        out_specs=(pl.BlockSpec(memory_space=pl.ANY),) * 2,
        scratch_shapes=[
            pltpu.SemaphoreType.DMA((2,)),
            pltpu.SemaphoreType.DMA((chips, 2)),
            pltpu.SemaphoreType.DMA((chips, 2)),
            pltpu.SemaphoreType.DMA((chips, 2)),
            pltpu.SemaphoreType.DMA((chips, 2)),
            pltpu.SemaphoreType.DMA((peers,)),
            pltpu.SemaphoreType.DMA((peers,)),
            pltpu.SemaphoreType.DMA(()),
        ],
        compiler_params=pltpu.CompilerParams(has_side_effects=True),
    )(block, rows)


def per_device(green, screened, cell_map, shift_table, shift_count):
    cell_count = lax.axis_size("cell")
    per_energy = green.shape[1]
    per_cell = green.shape[2]
    width = green.shape[4]
    flat = screened.reshape(4, per_energy, screened.shape[2], width)
    picked = jnp.take(flat, cell_map, axis=2, mode="clip")
    picked = picked.reshape(4, per_energy, cell_count, per_cell, width)
    outgoing = jnp.transpose(picked, (2, 0, 1, 3, 4)).reshape(cell_count, -1, width)
    whole, arrived = ring_gather(green, outgoing)
    arrived = arrived.reshape(cell_count, 4, per_energy, per_cell, width)
    owned = jnp.transpose(arrived, (1, 2, 3, 0, 4))
    group = lax.axis_index("energy")
    shifts, lives = slot_tables(shift_table, shift_count, group)
    return ring_convolve(shifts, lives, owned, whole, shift_table.shape[2])


def solution(mesh):
    placed = (
        P(None, "energy", "cell", None, None),
        P(None, "energy", None, "cell", None),
        P(),
        P(),
        P(),
    )
    return jax.shard_map(
        per_device,
        mesh=mesh,
        in_specs=placed,
        out_specs=P(None, "energy", "cell", None, None),
        check_vma=False,
    )
```

```python
import functools

import jax
import jax.numpy as jnp
from jax import lax
from jax.experimental import pallas as pl
from jax.experimental.pallas import tpu as pltpu
from jax.sharding import PartitionSpec as P

SCALE = 0.2
LANES = 128


def slot_tables(shift_table, shift_count, group):
    groups, slot_count = shift_table.shape[1], shift_table.shape[2]
    slot = lax.broadcasted_iota(jnp.int32, (groups, slot_count), 1)
    live = (slot < shift_count[group][:, None]).astype(jnp.float32)
    return shift_table[group].reshape(-1), live.reshape(-1)


def ring_conv_kernel(chips, slot_count, shift_ref, live_ref, w_hbm, g_hbm, o_ref, g_vmem, *scratch):
    halves = 2
    count = 2 * chips
    bufs = [scratch[h * count:(h + 1) * count] for h in range(halves)]
    own_bufs = [b[0] for b in bufs]
    ring_bufs = [(None,) + tuple(b[1:chips]) for b in bufs]
    hand_bufs = [tuple(b[chips:count]) for b in bufs]
    g_sem, local_sem, ring_send, ring_recv, pass_send, pass_recv = scratch[halves * count:]
    comps, per_energy, positions, rows, width = o_ref.shape
    me = lax.axis_index("energy")
    cell = lax.axis_index("cell")
    chip, core = me // 2, me % 2
    step_dir = 1 - 2 * core
    partner = me + step_dir
    ahead = 2 * ((chip + step_dir + chips) % chips) + core
    base = me * per_energy

    def origin(k):
        return 2 * ((chip - step_dir * k + chips) % chips) + core

    def handed_group(k):
        return 2 * ((chip + step_dir * k + chips) % chips) + 1 - core

    def own_half(h):
        return w_hbm.at[pl.ds(2 * h, 2)]

    def remote(src, dst, send, recv, k, h, target):
        return pltpu.make_async_remote_copy(
            src_ref=src, dst_ref=dst, send_sem=send.at[k, h], recv_sem=recv.at[k, h],
            device_id=(target, cell), device_id_type=pl.DeviceIdType.MESH,
        )

    def ring_copy(k, h):
        src = own_half(h) if k == 1 else ring_bufs[h][k - 1]
        return remote(src, ring_bufs[h][k], ring_send, ring_recv, k, h, ahead)

    def pass_copy(k, h):
        src = own_half(h) if k == 0 else ring_bufs[h][k]
        return remote(src, hand_bufs[h][k], pass_send, pass_recv, k, h, partner)

    def arrival(k, h):
        return remote(ring_bufs[h][k], ring_bufs[h][k], ring_send, ring_recv, k, h, ahead)

    def handed(k, h):
        return remote(hand_bufs[h][k], hand_bufs[h][k], pass_send, pass_recv, k, h, partner)

    def compute(source, buf, kind, masked):
        lag = base - source * per_energy

        def run():
            for p in range(positions):
                for chunk in range(width // LANES):
                    lanes = pl.ds(chunk * LANES, LANES)

                    def over_energy(e, carry, p=p, lanes=lanes):
                        real = jnp.zeros((rows, LANES), jnp.float32)
                        imag = jnp.zeros((rows, LANES), jnp.float32)
                        for c in range(slot_count):
                            j = shift_ref[source * slot_count + c]
                            weight = live_ref[source * slot_count + c]
                            u = lag + e - j
                            if masked:
                                weight = jnp.where(u >= 0, weight, 0.0)
                                u = jnp.maximum(u, 0)
                            gr = g_vmem[2 * kind, u, p, :, lanes].astype(jnp.float32)
                            gi = g_vmem[2 * kind + 1, u, p, :, lanes].astype(jnp.float32)
                            wr = buf[0, j, p, :, lanes].astype(jnp.float32) * weight
                            wi = buf[1, j, p, :, lanes].astype(jnp.float32) * weight
                            real = real - (gr * wi + gi * wr)
                            imag = imag + (gr * wr - gi * wi)
                        o_ref[2 * kind, e, p, :, lanes] += real
                        o_ref[2 * kind + 1, e, p, :, lanes] += imag
                        return carry

                    lax.fori_loop(0, per_energy, over_energy, 0)

        if masked:
            run()
        else:
            pl.when(source < me)(run)

    g_copy = pltpu.make_async_copy(g_hbm, g_vmem, g_sem)
    g_copy.start()
    locals_ = [pltpu.make_async_copy(own_half(h), own_bufs[h], local_sem.at[h]) for h in range(halves)]
    for copy in locals_:
        copy.start()
    sends = [ring_copy(1, h) for h in range(halves)] + [pass_copy(0, h) for h in range(halves)]
    for copy in sends:
        copy.start()
    o_ref[...] = jnp.zeros(o_ref.shape, o_ref.dtype)
    g_copy.wait()
    for h in range(halves):
        locals_[h].wait()
        compute(me, own_bufs[h], h, True)
    for k in range(1, chips):
        for h in range(halves):
            arrival(k, h).wait_recv()
            onward = [pass_copy(k, h)]
            if k + 1 < chips:
                onward.append(ring_copy(k + 1, h))
            for copy in onward:
                copy.start()
            sends.extend(onward)
            compute(origin(k), ring_bufs[h][k], h, False)
        for h in range(halves):
            handed(k - 1, h).wait_recv()
            compute(handed_group(k - 1), hand_bufs[h][k - 1], h, False)
    for h in range(halves):
        handed(chips - 1, h).wait_recv()
        compute(handed_group(chips - 1), hand_bufs[h][chips - 1], h, False)
    for copy in sends:
        copy.wait_send()
    o_ref[...] = o_ref[...] * SCALE


def ring_convolve(shifts, lives, owned, whole, slot_count):
    groups = lax.axis_size("energy")
    chips = groups // 2
    half = pltpu.VMEM((owned.shape[0] // 2,) + owned.shape[1:], owned.dtype)
    return pl.pallas_call(
        functools.partial(ring_conv_kernel, chips, slot_count),
        out_shape=jax.ShapeDtypeStruct(owned.shape, jnp.float32),
        in_specs=[
            pl.BlockSpec(memory_space=pltpu.SMEM),
            pl.BlockSpec(memory_space=pltpu.SMEM),
            pl.BlockSpec(memory_space=pl.ANY),
            pl.BlockSpec(memory_space=pl.ANY),
        ],
        out_specs=pl.BlockSpec(memory_space=pltpu.VMEM),
        scratch_shapes=[pltpu.VMEM(whole.shape, whole.dtype)]
        + [half] * (4 * chips)
        + [
            pltpu.SemaphoreType.DMA(()),
            pltpu.SemaphoreType.DMA((2,)),
            pltpu.SemaphoreType.DMA((chips, 2)),
            pltpu.SemaphoreType.DMA((chips, 2)),
            pltpu.SemaphoreType.DMA((chips, 2)),
            pltpu.SemaphoreType.DMA((chips, 2)),
        ],
        compiler_params=pltpu.CompilerParams(
            has_side_effects=True, vmem_limit_bytes=48 * 1024 * 1024
        ),
    )(shifts, lives, owned, whole)


def gather_kernel(chips, x_hbm, rows_hbm, out_ref, owned_ref, local_sem, ring_send, ring_recv,
                  pass_send, pass_recv, row_send, row_recv, row_local):
    halves = 2
    per_energy = x_hbm.shape[1]
    me = lax.axis_index("energy")
    cell = lax.axis_index("cell")
    chip, core = me // 2, me % 2
    step_dir = 1 - 2 * core
    partner = me + step_dir
    ahead = 2 * ((chip + step_dir + chips) % chips) + core

    def origin(k):
        return 2 * ((chip - step_dir * k + chips) % chips) + core

    def handed_group(k):
        return 2 * ((chip + step_dir * k + chips) % chips) + 1 - core

    def place(group, h):
        return out_ref.at[pl.ds(2 * h, 2), pl.ds(group * per_energy, per_energy)]

    def own_half(h):
        return x_hbm.at[pl.ds(2 * h, 2)]

    def remote(src, dst, send, recv, k, h, target):
        return pltpu.make_async_remote_copy(
            src_ref=src, dst_ref=dst, send_sem=send.at[k, h], recv_sem=recv.at[k, h],
            device_id=(target, cell), device_id_type=pl.DeviceIdType.MESH,
        )

    def ring_copy(k, h):
        src = own_half(h) if k == 1 else place(origin(k - 1), h)
        return remote(src, place(origin(k - 1), h), ring_send, ring_recv, k, h, ahead)

    def pass_copy(k, h):
        src = own_half(h) if k == 0 else place(origin(k), h)
        return remote(src, place(origin(k), h), pass_send, pass_recv, k, h, partner)

    def arrival(k, h):
        return remote(place(origin(k), h), place(origin(k), h), ring_send, ring_recv, k, h, ahead)

    def handed(k, h):
        slot = place(handed_group(k), h)
        return remote(slot, slot, pass_send, pass_recv, k, h, partner)

    peers = rows_hbm.shape[0]

    def row_copy(d):
        return pltpu.make_async_remote_copy(
            src_ref=rows_hbm.at[d],
            dst_ref=owned_ref.at[cell],
            send_sem=row_send.at[d], recv_sem=row_recv.at[cell],
            device_id=(me, d), device_id_type=pl.DeviceIdType.MESH,
        )

    def row_arrival(r):
        return pltpu.make_async_remote_copy(
            src_ref=owned_ref.at[r],
            dst_ref=owned_ref.at[r],
            send_sem=row_send.at[r], recv_sem=row_recv.at[r],
            device_id=(me, r), device_id_type=pl.DeviceIdType.MESH,
        )

    own_rows = pltpu.make_async_copy(
        rows_hbm.at[cell], owned_ref.at[cell], row_local
    )
    own_rows.start()
    row_sends = []
    for step in range(1, peers):
        copy = row_copy((cell + step) % peers)
        copy.start()
        row_sends.append(copy)

    locals_ = [pltpu.make_async_copy(own_half(h), place(me, h), local_sem.at[h]) for h in range(halves)]
    for copy in locals_:
        copy.start()
    sends = [ring_copy(1, h) for h in range(halves)] + [pass_copy(0, h) for h in range(halves)]
    for copy in sends:
        copy.start()
    for k in range(1, chips):
        for h in range(halves):
            arrival(k, h).wait_recv()
            onward = [pass_copy(k, h)]
            if k + 1 < chips:
                onward.append(ring_copy(k + 1, h))
            for copy in onward:
                copy.start()
            sends.extend(onward)
    for k in range(chips):
        for h in range(halves):
            handed(k, h).wait_recv()
    for step in range(1, peers):
        row_arrival((cell + peers - step) % peers).wait_recv()
    for copy in row_sends:
        copy.wait_send()
    own_rows.wait()
    for copy in sends:
        copy.wait_send()
    for copy in locals_:
        copy.wait()


def ring_gather(block, rows):
    groups = lax.axis_size("energy")
    peers = lax.axis_size("cell")
    chips = groups // 2
    shape = (block.shape[0], groups * block.shape[1]) + block.shape[2:]
    return pl.pallas_call(
        functools.partial(gather_kernel, chips),
        out_shape=(
            jax.ShapeDtypeStruct(shape, block.dtype),
            jax.ShapeDtypeStruct(rows.shape, rows.dtype),
        ),
        in_specs=[pl.BlockSpec(memory_space=pl.ANY)] * 2,
        out_specs=(pl.BlockSpec(memory_space=pl.ANY),) * 2,
        scratch_shapes=[
            pltpu.SemaphoreType.DMA((2,)),
            pltpu.SemaphoreType.DMA((chips, 2)),
            pltpu.SemaphoreType.DMA((chips, 2)),
            pltpu.SemaphoreType.DMA((chips, 2)),
            pltpu.SemaphoreType.DMA((chips, 2)),
            pltpu.SemaphoreType.DMA((peers,)),
            pltpu.SemaphoreType.DMA((peers,)),
            pltpu.SemaphoreType.DMA(()),
        ],
        compiler_params=pltpu.CompilerParams(has_side_effects=True),
    )(block, rows)


def per_device(green, screened, cell_map, shift_table, shift_count):
    cell_count = lax.axis_size("cell")
    per_energy = green.shape[1]
    per_cell = green.shape[2]
    width = green.shape[4]
    flat = screened.reshape(4, per_energy, screened.shape[2], width)
    picked = jnp.take(flat, cell_map, axis=2, mode="clip")
    picked = picked.reshape(4, per_energy, cell_count, per_cell, width)
    outgoing = jnp.transpose(picked, (2, 0, 1, 3, 4))
    whole, arrived = ring_gather(green, outgoing)
    arrived = arrived.reshape(cell_count, 4, per_energy, per_cell, width)
    owned = jnp.transpose(arrived, (1, 2, 3, 0, 4))
    group = lax.axis_index("energy")
    shifts, lives = slot_tables(shift_table, shift_count, group)
    return ring_convolve(shifts, lives, owned, whole, shift_table.shape[2])


def solution(mesh):
    placed = (
        P(None, "energy", "cell", None, None),
        P(None, "energy", None, "cell", None),
        P(),
        P(),
        P(),
    )
    return jax.shard_map(
        per_device,
        mesh=mesh,
        in_specs=placed,
        out_specs=P(None, "energy", "cell", None, None),
        check_vma=False,
    )
```
